32 devices in a mesh: gx: 4 (over y, x), gy: 4 (over z), gz: 2 (over core).
Axes of the slice: x: 2, y: 2, z: 4, core: 2. Of those that a mesh axis runs over, the one named last changes fastest.
Arguments:
- points: float32 [65536, 512], P(('gx', 'gy', 'gz')), may hold values from -6 to 6
- order: int32 [65536], P(('gx', 'gy', 'gz')), may hold values from 0 to 65535, as said below
- near: bfloat16 [64, 1024, 1024], P(('gx', 'gy', 'gz')), may hold values from -0.1875 to 0.1875
- basis_in: bfloat16 [64, 1024, 256], P(('gx', 'gy', 'gz')), may hold values from -0.1875 to 0.1875
- basis_out: bfloat16 [64, 1024, 256], P(('gx', 'gy', 'gz')), may hold values from -0.375 to 0.375
- leaf_coupling: bfloat16 [64, 3, 256, 256], P(('gx', 'gy', 'gz')), may hold values from -0.375 to 0.375
- transfer_up: bfloat16 [32, 2, 1024, 256], P(('gx', 'gy', 'gz')), may hold values from -0.09375 to 0.09375, as said below
- transfer_down: bfloat16 [32, 2, 1024, 256], P(('gx', 'gy', 'gz')), may hold values from -0.1875 to 0.1875, as said below
- node_coupling: bfloat16 [32, 2, 3, 256, 256], P(('gx', 'gy', 'gz')), may hold values from -0.1875 to 0.1875, as said below
- ridge: float32 [1], replicated, may hold values from 0.5 to 2
Outputs:
- result: float32 [65536, 512], P(('gx', 'gy', 'gz'))
The draws below stay inside these ranges and needn't reach their ends.
Inputs may be any that keep to these rules, and one draw needn't show every extreme that they name: `order`: each device's 2048 consecutive entries are a permutation of the initial indices of those same rows. `transfer_up`: rows d and e are equal at level k whenever devices d and e have the same ancestor at level k. `transfer_down`: rows d and e are equal at level k whenever devices d and e have the same ancestor at level k. `node_coupling`: rows d and e are equal at level k whenever devices d and e have the same ancestor at level k.
All inputs are finite; a program needn't handle non-finite values.
Results may differ from the reference program's by a relative error of at most 0.014.
Values may be sent and summed in bfloat16 or wider, within the bound.
No kernel may reach another device: no remote copies, remote signals or barrier semaphores. Data moves between devices by JAX's collectives and lax.ppermute only.
A program may use at most 128 MiB of HBM per device.

```python
import math
import jax
import jax.numpy as jnp
import numpy as np
from jax import lax

LEAF = 1024
RANK = 256
COLS = 512
LEAF_DEV = 2
LEAVES = 64
ROWS_DEV = 2048
POINTS = 65536
LEVELS = 3


def path_tables(key, tail, fan):
    device_count = LEAVES // LEAF_DEV
    devices_all = jnp.arange(device_count)
    stacked = []
    for height in range(1, LEVELS):
        nodes = LEAVES // 4 ** height
        level_key = jax.random.fold_in(key, height)
        table = jnp.clip(jax.random.normal(level_key, (nodes,) + tail, jnp.float32), -3.0, 3.0)
        stacked.append(table[LEAF_DEV * devices_all // 4 ** height] / math.sqrt(fan))
    return jnp.stack(stacked, axis=1)


def draw_transfer_up(key, part):
    return path_tables(jax.random.fold_in(key, 11), (4 * RANK, RANK), 4 * RANK).astype(jnp.bfloat16)


def draw_transfer_down(key, part):
    return path_tables(jax.random.fold_in(key, 23), (4 * RANK, RANK), RANK).astype(jnp.bfloat16)


def draw_node_coupling(key, part):
    return path_tables(jax.random.fold_in(key, 37), (3, RANK, RANK), RANK).astype(jnp.bfloat16)


def permute_block(block_key):
    return jax.random.permutation(block_key, ROWS_DEV)


def draw_order(key, part):
    device_count = POINTS // ROWS_DEV
    block_keys = jax.random.split(key, device_count)
    blocks = jax.vmap(permute_block)(block_keys)
    offsets = jnp.arange(device_count, dtype=jnp.int32)[:, None] * ROWS_DEV
    return (blocks.astype(jnp.int32) + offsets).reshape(POINTS).astype(jnp.int32)


def level_of(rng, shape, shards, least, largest):
    factor_of = 1.0
    for dim, blocks in shards:
        steps = jax.random.uniform(jax.random.fold_in(jax.random.fold_in(rng, 6), dim), (blocks,), jnp.float32, least / len(shards), largest / len(shards))
        factor_of = factor_of * jnp.repeat(jnp.exp(steps), shape[dim] // blocks).reshape((-1,) + (1,) * (len(shape) - 1 - dim))
    return factor_of


def noise(key, extent, width, most, shards=(), kind=jnp.bfloat16):
    loudness = level_of(key, extent, shards, -0.22, 0.18) if shards else 1.0
    values = jax.random.normal(key, extent, jnp.float32) * width * loudness
    return jnp.minimum(jnp.maximum(values, -most), most).astype(kind)


def setup_inputs(seed: int = 0) -> dict:
    seeds = jax.random.split(jax.random.key(seed), 11)
    points = noise(seeds[0], (POINTS, COLS), 1.0, 6.0, ((0, 32),), jnp.float32)
    order = draw_order(jax.random.fold_in(seeds[10], 71), 0)
    near = noise(seeds[2], (LEAVES, LEAF, LEAF), LEAF ** -0.5, 0.1875, ((0, 32),))
    basis_in = noise(seeds[3], (LEAVES, LEAF, RANK), LEAF ** -0.5, 0.1875, ((0, 32),))
    basis_out = noise(seeds[4], (LEAVES, LEAF, RANK), RANK ** -0.5, 0.375, ((0, 32),))
    leaf_coupling = noise(seeds[5], (LEAVES, 3, RANK, RANK), RANK ** -0.5, 0.375, ((0, 32),))
    transfer_up = draw_transfer_up(jax.random.fold_in(seeds[10], 71), 0)
    transfer_down = draw_transfer_down(jax.random.fold_in(seeds[10], 71), 0)
    node_coupling = draw_node_coupling(jax.random.fold_in(seeds[10], 71), 0)
    ridge = jnp.clip(jax.random.uniform(seeds[9], (1,), jnp.float32, 0.5, 2.0), 0.5, 2.0)
    return dict(points=points, order=order, near=near, basis_in=basis_in, basis_out=basis_out, leaf_coupling=leaf_coupling, transfer_up=transfer_up, transfer_down=transfer_down, node_coupling=node_coupling, ridge=ridge)


SIBLINGS = np.array([[1, 2, 3], [0, 2, 3], [0, 1, 3], [0, 1, 2]], dtype=np.int32)


def couple(node_hats, coupling):
    count = node_hats.shape[0]
    grouped = node_hats.reshape(count // 4, 4, node_hats.shape[1], node_hats.shape[2])
    others = grouped[:, SIBLINGS].reshape(count, 3, node_hats.shape[1], node_hats.shape[2])
    return jnp.einsum('njrs,njsc->nrc', coupling.astype(jnp.float32), others.astype(jnp.float32))


def leaf_up(leaf_items):
    return jnp.dot(leaf_items[0].T, leaf_items[1], preferred_element_type=jnp.float32).astype(jnp.bfloat16)


def leaf_out(leaf_items):
    dense_block, out_basis, values, far_rows = leaf_items
    return jnp.dot(dense_block, values, preferred_element_type=jnp.float32) + jnp.dot(out_basis, far_rows, preferred_element_type=jnp.float32)


def reference(points, order, near, basis_in, basis_out, leaf_coupling, transfer_up, transfer_down, node_coupling, ridge):
    ordered = jnp.take(points, order.astype(jnp.int32), axis=0)
    rounded = ordered.astype(jnp.bfloat16).reshape(LEAVES, LEAF, COLS)
    node_hats = [lax.map(leaf_up, (basis_in, rounded))]
    for height in range(1, LEVELS):
        stride = 4 ** height // LEAF_DEV
        lifters = transfer_up[::stride, height - 1]
        below_hats = node_hats[-1].reshape(lifters.shape[0], 4 * RANK, COLS)
        lifted = jnp.einsum('nkr,nkc->nrc', lifters.astype(jnp.float32), below_hats.astype(jnp.float32))
        node_hats.append(lifted.astype(jnp.bfloat16))
    far_terms = [couple(node_hats[0], leaf_coupling)]
    for height in range(1, LEVELS):
        stride = 4 ** height // LEAF_DEV
        far_terms.append(couple(node_hats[height], node_coupling[::stride, height - 1]))
    down_value = far_terms[LEVELS - 1]
    for height in range(LEVELS - 2, -1, -1):
        stride = 4 ** (height + 1) // LEAF_DEV
        lowers = transfer_down[::stride, height]
        parent_rows = lax.optimization_barrier(down_value.astype(jnp.bfloat16)).astype(jnp.float32)
        spread = jnp.einsum('nkr,nrc->nkc', lowers.astype(jnp.float32), parent_rows)
        down_value = far_terms[height] + spread.reshape(-1, RANK, COLS)
    lowered = down_value.astype(jnp.bfloat16)
    tree_out = lax.map(leaf_out, (near, basis_out, rounded, lowered))
    tree_out = tree_out + ridge[0] * ordered.reshape(LEAVES, LEAF, COLS)
    return jnp.zeros_like(points).at[order.astype(jnp.int32)].set(tree_out.reshape(POINTS, COLS))
```

```python
import jax
import jax.numpy as jnp
from jax import lax
from jax.experimental import pallas as pl
from jax.experimental.pallas import tpu as pltpu
from jax.sharding import PartitionSpec as P

LANES = 128
ARITY = 4
MIB = 1 << 20


def vmem_spec():
    return pl.BlockSpec(memory_space=pltpu.VMEM)


def dot(left, right):
    return jnp.dot(left, right, preferred_element_type=jnp.float32)


def dot_t(left, right):
    return lax.dot_general(
        left, right, (((0,), (0,)), ((), ())), preferred_element_type=jnp.float32
    )


def local_row(value, rows):
    if rows & (rows - 1) == 0:
        return value & (rows - 1)
    return lax.rem(value, rows)


def fixed(value):
    return lambda: jnp.int32(value)


def slot_of(axis, shift):
    return (lax.axis_index(axis) >> shift) & (ARITY - 1)


def sibling(slot, step):
    other = slot ^ step
    return other, other - (other > slot).astype(jnp.int32)


def upward_leaves(points, order, basis_in, held):
    rows, columns = points.shape
    leaves, leaf_rows, rank = basis_in.shape
    tiles = columns // LANES
    parts = 4
    step = rows // parts
    unroll = 16

    def body(*refs):
        order_ref, points_ref, basis_hbm = refs[:3]
        held_in = refs[3 : 3 + len(held)]
        outs = refs[3 + len(held) :]
        rounded_ref, hat_ref, ordered_ref = outs[:3]
        held_out = outs[3 : 3 + len(held)]
        plain, tiled, basis_ref, sems, basis_sem, held_sems = outs[3 + len(held) :]
        copies = [
            pltpu.make_async_copy(
                points_ref.at[pl.ds(p * step, step), :],
                plain.at[pl.ds(p * step, step), :],
                sems.at[p],
            )
            for p in range(parts)
        ]
        for copy in copies:
            copy.start()
        basis_copy = pltpu.make_async_copy(basis_hbm, basis_ref, basis_sem)
        basis_copy.start()
        held_copies = [
            pltpu.make_async_copy(src, dst, held_sems.at[i])
            for i, (src, dst) in enumerate(zip(held_in, held_out))
        ]
        for p, copy in enumerate(copies):
            copy.wait()
            for t in range(tiles):
                tiled[p * step : (p + 1) * step, t, :] = plain[
                    p * step : (p + 1) * step, t * LANES : (t + 1) * LANES
                ]
        for copy in held_copies:
            copy.start()

        def move(block, _):
            base = pl.multiple_of(block * unroll, unroll)
            for u in range(unroll):
                ordered_ref[base + u] = tiled[local_row(order_ref[base + u], rows)]
            return 0

        lax.fori_loop(0, rows // unroll, move, 0)
        flat = ordered_ref.reshape(rows * tiles, LANES)
        chunk = 256

        def spread(block, _):
            base = pl.multiple_of(block * chunk, chunk)
            for t in range(tiles):
                rounded_ref[pl.ds(base, chunk), t * LANES : (t + 1) * LANES] = flat[
                    pl.ds(base * tiles + t, chunk, stride=tiles), :
                ].astype(jnp.bfloat16)
            return 0

        lax.fori_loop(0, rows // chunk, spread, 0)
        basis_copy.wait()
        for leaf in range(leaves):
            hat_ref[leaf] = dot_t(
                basis_ref[leaf], rounded_ref[leaf * leaf_rows : (leaf + 1) * leaf_rows, :]
            ).astype(jnp.bfloat16)
        for copy in held_copies:
            copy.wait()

    any_spec = pl.BlockSpec(memory_space=pl.ANY)
    return pl.pallas_call(
        body,
        name="upward_leaves",
        out_shape=[
            pltpu.VMEM((rows, columns), jnp.bfloat16),
            pltpu.VMEM((leaves, rank, columns), jnp.bfloat16),
            pltpu.VMEM((rows, tiles, LANES), jnp.float32),
        ]
        + [pltpu.VMEM(h.shape, h.dtype) for h in held],
        in_specs=[pl.BlockSpec(memory_space=pltpu.SMEM)] + [any_spec] * (2 + len(held)),
        out_specs=[vmem_spec()] * (3 + len(held)),
        scratch_shapes=[
            pltpu.VMEM((rows, columns), jnp.float32),
            pltpu.VMEM((rows, tiles, LANES), jnp.float32),
            pltpu.VMEM(basis_in.shape, basis_in.dtype),
            pltpu.SemaphoreType.DMA((parts,)),
            pltpu.SemaphoreType.DMA,
            pltpu.SemaphoreType.DMA((len(held),)),
        ],
        compiler_params=pltpu.CompilerParams(vmem_limit_bytes=30 * MIB),
    )(order, points, basis_in, *held)


def call_small(body, name, out_shape, operands, scratch=(), limit=16):
    many = isinstance(out_shape, list)
    return pl.pallas_call(
        body,
        name=name,
        out_shape=out_shape,
        in_specs=[vmem_spec()] * len(operands),
        out_specs=[vmem_spec()] * len(out_shape) if many else vmem_spec(),
        scratch_shapes=list(scratch),
        compiler_params=pltpu.CompilerParams(vmem_limit_bytes=limit * MIB),
    )(*operands)


def first_lift(own, partner, lifters):
    leaves, rank, columns = own.shape
    half = columns // 2

    def body(own_ref, partner_ref, lifter_ref, out_ref):
        low = lax.axis_index("gz") & 1
        total = None
        cols = pl.ds(pl.multiple_of(low * half, half), half)
        for source, place in ((own_ref, low), (partner_ref, 1 - low)):
            for leaf in range(leaves):
                first = pl.multiple_of((place * leaves + leaf) * rank, rank)
                term = dot_t(lifter_ref[0, 0, pl.ds(first, rank), :], source[leaf, :, cols])
                total = term if total is None else total + term
        out_ref[...] = total.astype(jnp.bfloat16)

    return call_small(
        body, "first_lift", pltpu.VMEM((rank, half), jnp.bfloat16), [own, partner, lifters]
    )


def next_lift(own, others, lifters, stage, axis, shift):
    rank, half = own.shape

    def body(own_ref, a_ref, b_ref, c_ref, lifter_ref, out_ref):
        slot = slot_of(axis, shift)
        total = None
        for step, source in enumerate((own_ref, a_ref, b_ref, c_ref)):
            first = pl.multiple_of((slot ^ step) * rank, rank)
            term = dot_t(lifter_ref[0, stage + 1, pl.ds(first, rank), :], source[...])
            total = term if total is None else total + term
        out_ref[...] = total.astype(jnp.bfloat16)

    return call_small(
        body, "next_lift", pltpu.VMEM((rank, half), jnp.bfloat16), [own, *others, lifters]
    )


def far_sum(sources, coupling_ref, stage, slot):
    total = None
    for step, source in enumerate(sources, 1):
        _, place = sibling(slot, step)
        term = dot(coupling_ref[0, stage, place], source[...])
        total = term if total is None else total + term
    return total


def far_of(others, couplings, stage, axis, shift, after):
    rank, half = others[0].shape

    def body(a_ref, b_ref, c_ref, coupling_ref, after_ref, out_ref):
        out_ref[...] = far_sum(
            (a_ref, b_ref, c_ref), coupling_ref, stage, slot_of(axis, shift)
        )

    return call_small(
        body, "far_of", pltpu.VMEM((rank, half), jnp.float32), [*others, couplings, after]
    )


def go_down(others, fars, couplings, lowers, places):
    rank, half = others[0].shape
    top = len(places) - 1

    def body(*refs):
        a_ref, b_ref, c_ref, coupling_ref, lower_ref = refs[:5]
        far_refs = refs[5:-1]
        value = far_sum((a_ref, b_ref, c_ref), coupling_ref, top, slot_of(*places[top]))
        for stage in range(top - 1, -1, -1):
            first = pl.multiple_of(slot_of(*places[stage]) * rank, rank)
            block = lower_ref[0, stage + 1, pl.ds(first, rank), :]
            value = far_refs[stage][...] + dot(block, value.astype(jnp.bfloat16))
        refs[-1][...] = value.astype(jnp.bfloat16)

    return call_small(
        body,
        "go_down",
        pltpu.VMEM((rank, half), jnp.bfloat16),
        [*others, couplings, lowers, *fars],
    )


def local_part(
    rounded, ordered, own, partner, near, basis_out, leaf_coupling, lowers, order, ridge, after
):
    rows, columns = rounded.shape
    leaves, leaf_rows, _ = near.shape
    rank = basis_out.shape[2]
    tiles = columns // LANES
    rank_tiles = rank // LANES
    width = -(-(tiles + rank_tiles) // 8) * 8
    chunk = 256
    unroll = 16

    def body(
        order_ref,
        ridge_ref,
        rounded_ref,
        ordered_ref,
        own_ref,
        partner_ref,
        near_ref,
        basis_ref,
        coupling_ref,
        lower_ref,
        after_ref,
        base_ref,
        spread_ref,
        children,
        tree,
        initial,
    ):
        low = lax.axis_index("gz") & 1
        ridge_value = ridge_ref[0]
        children[pl.ds(low * leaves, leaves)] = own_ref[...]
        children[pl.ds((1 - low) * leaves, leaves)] = partner_ref[...]
        tree_flat = tree.reshape(rows * width, LANES)
        ordered_flat = ordered_ref.reshape(rows * tiles, LANES)
        initial_flat = initial.reshape(rows * width, LANES)
        for leaf in range(leaves):
            slot = low * leaves + leaf
            far = None
            for t in range(ARITY - 1):
                source = t + (t >= slot).astype(jnp.int32)
                term = dot(coupling_ref[leaf, t], children[source])
                far = term if far is None else far + term
            far = far.astype(jnp.bfloat16)
            first = pl.multiple_of(slot * rank, rank)
            lower = lower_ref[0, 0, pl.ds(first, rank), :]
            values = rounded_ref[leaf * leaf_rows : (leaf + 1) * leaf_rows, :]

            def tile(block, _):
                inner = pl.multiple_of(block * chunk, chunk)
                outer = inner + leaf * leaf_rows
                basis = basis_ref[leaf, pl.ds(inner, chunk), :]
                value = dot(near_ref[leaf, pl.ds(inner, chunk), :], values) + dot(basis, far)
                for t in range(tiles):
                    kept = ordered_flat[pl.ds(outer * tiles + t, chunk, stride=tiles), :]
                    tree_flat[pl.ds(outer * width + t, chunk, stride=width), :] = (
                        value[:, t * LANES : (t + 1) * LANES] + ridge_value * kept
                    )
                span = dot(basis, lower)
                for t in range(rank_tiles):
                    tree_flat[pl.ds(outer * width + tiles + t, chunk, stride=width), :] = span[
                        :, t * LANES : (t + 1) * LANES
                    ]
                return 0

            lax.fori_loop(0, leaf_rows // chunk, tile, 0)

        def move(block, _):
            base = pl.multiple_of(block * unroll, unroll)
            for u in range(unroll):
                initial[local_row(order_ref[base + u], rows)] = tree[base + u]
            return 0

        lax.fori_loop(0, rows // unroll, move, 0)

        def spread(block, _):
            base = pl.multiple_of(block * chunk, chunk)
            for t in range(tiles):
                base_ref[pl.ds(base, chunk), t * LANES : (t + 1) * LANES] = initial_flat[
                    pl.ds(base * width + t, chunk, stride=width), :
                ]
            for t in range(rank_tiles):
                spread_ref[pl.ds(base, chunk), t * LANES : (t + 1) * LANES] = initial_flat[
                    pl.ds(base * width + tiles + t, chunk, stride=width), :
                ].astype(jnp.bfloat16)
            return 0

        lax.fori_loop(0, rows // chunk, spread, 0)

    smem = pl.BlockSpec(memory_space=pltpu.SMEM)
    return pl.pallas_call(
        body,
        name="local_part",
        out_shape=[
            pltpu.VMEM((rows, columns), jnp.float32),
            pltpu.VMEM((rows, rank), jnp.bfloat16),
        ],
        in_specs=[smem, smem] + [vmem_spec()] * 9,
        out_specs=[vmem_spec()] * 2,
        scratch_shapes=[
            pltpu.VMEM((ARITY, rank, columns), jnp.bfloat16),
            pltpu.VMEM((rows, width, LANES), jnp.float32),
            pltpu.VMEM((rows, width, LANES), jnp.float32),
        ],
        compiler_params=pltpu.CompilerParams(vmem_limit_bytes=40 * MIB),
    )(
        order,
        ridge,
        rounded,
        ordered,
        own,
        partner,
        near,
        basis_out,
        leaf_coupling,
        lowers,
        after,
    )


def finish(base, spread, own, partner):
    rows, columns = base.shape
    rank, half = own.shape
    parts = 8
    step = rows // parts

    def body(base_ref, spread_ref, own_ref, partner_ref, out_ref, low_ref, result, sems):
        low = lax.axis_index("gz") & 1
        low_ref[:, pl.ds(pl.multiple_of(low * half, half), half)] = own_ref[...]
        low_ref[:, pl.ds(pl.multiple_of((1 - low) * half, half), half)] = partner_ref[...]
        copies = []
        for p in range(parts):
            piece = slice(p * step, (p + 1) * step)
            result[piece, :] = base_ref[piece, :] + dot(spread_ref[piece, :], low_ref[...])
            copy = pltpu.make_async_copy(
                result.at[pl.ds(p * step, step), :],
                out_ref.at[pl.ds(p * step, step), :],
                sems.at[p],
            )
            copy.start()
            copies.append(copy)
        for copy in copies:
            copy.wait()

    return pl.pallas_call(
        body,
        name="finish",
        out_shape=jax.ShapeDtypeStruct((rows, columns), jnp.float32),
        in_specs=[vmem_spec()] * 4,
        out_specs=pl.BlockSpec(memory_space=pl.ANY),
        scratch_shapes=[
            pltpu.VMEM((rank, columns), jnp.bfloat16),
            pltpu.VMEM((rows, columns), jnp.float32),
            pltpu.SemaphoreType.DMA((parts,)),
        ],
        compiler_params=pltpu.CompilerParams(vmem_limit_bytes=16 * MIB),
    )(base, spread, own, partner)


def swap(value, axis, mask):
    size = lax.axis_size(axis)
    return lax.ppermute(value, axis, [(s, s ^ mask) for s in range(size)])


def on_device(
    points,
    order,
    near,
    basis_in,
    basis_out,
    leaf_coupling,
    transfer_up,
    transfer_down,
    node_coupling,
    ridge,
):
    stages = transfer_up.shape[1]
    places = [("gz", 1 + 2 * i) for i in range(stages - 2)] + [("gy", 0), ("gx", 0)]
    held = [transfer_up, node_coupling, transfer_down, leaf_coupling, basis_out, near]
    rounded, leaf_hat, ordered, *kept = upward_leaves(points, order, basis_in, held)
    lifters, couplings, lowers, leaf_couplings, bases, blocks = kept
    partner_hat = swap(leaf_hat, "gz", 1)
    hat = first_lift(leaf_hat, partner_hat, lifters)
    base = spread = None
    fars = []
    for stage, (axis, shift) in enumerate(places):
        others = [swap(hat, axis, step << shift) for step in (1, 2, 3)]
        if base is None:
            base, spread = local_part(
                rounded,
                ordered,
                leaf_hat,
                partner_hat,
                blocks,
                bases,
                leaf_couplings,
                lowers,
                order,
                ridge,
                hat,
            )
        if stage + 1 < stages:
            hat = next_lift(hat, others, lifters, stage, axis, shift)
            fars.append(far_of(others, couplings, stage, axis, shift, hat))
    value = go_down(others, fars, couplings, lowers, places)
    partner_value = swap(value, "gz", 1)
    return finish(base, spread, value, partner_value)


def solution(mesh):
    placed = (
        P(("gx", "gy", "gz"), None),
        P(("gx", "gy", "gz")),
        P(("gx", "gy", "gz"), None, None),
        P(("gx", "gy", "gz"), None, None),
        P(("gx", "gy", "gz"), None, None),
        P(("gx", "gy", "gz"), None, None, None),
        P(("gx", "gy", "gz"), None, None, None),
        P(("gx", "gy", "gz"), None, None, None),
        P(("gx", "gy", "gz"), None, None, None, None),
        P(),
    )
    return jax.shard_map(
        on_device,
        mesh=mesh,
        in_specs=placed,
        out_specs=P(("gx", "gy", "gz"), None),
        check_vma=False,
    )
```

```python
import jax
import jax.numpy as jnp
from jax import lax
from jax.experimental import pallas as pl
from jax.experimental.pallas import tpu as pltpu
from jax.sharding import PartitionSpec as P

LANES = 128
ARITY = 4
MIB = 1 << 20


def vmem_spec():
    return pl.BlockSpec(memory_space=pltpu.VMEM)


def stay(value):
    return pltpu.with_memory_space_constraint(value, pltpu.HBM)


def dot(left, right):
    return jnp.dot(left, right, preferred_element_type=jnp.float32)


def dot_t(left, right):
    return lax.dot_general(
        left, right, (((0,), (0,)), ((), ())), preferred_element_type=jnp.float32
    )


def local_row(value, rows):
    if rows & (rows - 1) == 0:
        return value & (rows - 1)
    return lax.rem(value, rows)


def slot_of(axis, shift):
    return (lax.axis_index(axis) >> shift) & (ARITY - 1)


def sibling(slot, step):
    other = slot ^ step
    return other, other - (other > slot).astype(jnp.int32)


def upward_leaves(points, order, basis_in, held):
    rows, columns = points.shape
    leaves, leaf_rows, rank = basis_in.shape
    tiles = columns // LANES
    parts = 4
    step = rows // parts
    unroll = 16

    def body(*refs):
        order_hbm, points_ref, basis_hbm = refs[:3]
        held_in = refs[3 : 3 + len(held)]
        outs = refs[3 + len(held) :]
        rounded_ref, hat_ref, ordered_ref = outs[:3]
        held_out = outs[3 : 3 + len(held)]
        plain, tiled, basis_ref, order_ref, sems, basis_sem, order_sem, held_sems = outs[
            3 + len(held) :
        ]
        order_copy = pltpu.make_async_copy(order_hbm, order_ref, order_sem)
        order_copy.start()
        copies = [
            pltpu.make_async_copy(
                points_ref.at[pl.ds(p * step, step), :],
                plain.at[pl.ds(p * step, step), :],
                sems.at[p],
            )
            for p in range(parts)
        ]
        for copy in copies:
            copy.start()
        basis_copy = pltpu.make_async_copy(basis_hbm, basis_ref, basis_sem)
        basis_copy.start()
        held_copies = [
            pltpu.make_async_copy(src, dst, held_sems.at[i])
            for i, (src, dst) in enumerate(zip(held_in, held_out))
        ]
        for p, copy in enumerate(copies):
            copy.wait()
            for t in range(tiles):
                tiled[p * step : (p + 1) * step, t, :] = plain[
                    p * step : (p + 1) * step, t * LANES : (t + 1) * LANES
                ]
        for copy in held_copies:
            copy.start()
        order_copy.wait()

        def move(block, _):
            base = pl.multiple_of(block * unroll, unroll)
            for u in range(unroll):
                ordered_ref[base + u] = tiled[local_row(order_ref[base + u], rows)]
            return 0

        lax.fori_loop(0, rows // unroll, move, 0)
        flat = ordered_ref.reshape(rows * tiles, LANES)
        chunk = 256

        def spread(block, _):
            base = pl.multiple_of(block * chunk, chunk)
            for t in range(tiles):
                rounded_ref[pl.ds(base, chunk), t * LANES : (t + 1) * LANES] = flat[
                    pl.ds(base * tiles + t, chunk, stride=tiles), :
                ].astype(jnp.bfloat16)
            return 0

        lax.fori_loop(0, rows // chunk, spread, 0)
        basis_copy.wait()
        for leaf in range(leaves):
            hat_ref[leaf] = dot_t(
                basis_ref[leaf], rounded_ref[leaf * leaf_rows : (leaf + 1) * leaf_rows, :]
            ).astype(jnp.bfloat16)
        for copy in held_copies:
            copy.wait()

    hbm_spec = pl.BlockSpec(memory_space=pltpu.HBM)
    return pl.pallas_call(
        body,
        name="upward_leaves",
        out_shape=[
            pltpu.VMEM((rows, columns), jnp.bfloat16),
            pltpu.VMEM((leaves, rank, columns), jnp.bfloat16),
            pltpu.VMEM((rows, tiles, LANES), jnp.float32),
        ]
        + [pltpu.VMEM(h.shape, h.dtype) for h in held],
        in_specs=[hbm_spec] * (3 + len(held)),
        out_specs=[vmem_spec()] * (3 + len(held)),
        scratch_shapes=[
            pltpu.VMEM((rows, columns), jnp.float32),
            pltpu.VMEM((rows, tiles, LANES), jnp.float32),
            pltpu.VMEM(basis_in.shape, basis_in.dtype),
            pltpu.SMEM(order.shape, order.dtype),
            pltpu.SemaphoreType.DMA((parts,)),
            pltpu.SemaphoreType.DMA,
            pltpu.SemaphoreType.DMA,
            pltpu.SemaphoreType.DMA((len(held),)),
        ],
        compiler_params=pltpu.CompilerParams(vmem_limit_bytes=12 * MIB),
    )(*[stay(value) for value in (order, points, basis_in, *held)])


def call_small(body, name, out_shape, operands, scratch=(), limit=4):
    many = isinstance(out_shape, list)
    return pl.pallas_call(
        body,
        name=name,
        out_shape=out_shape,
        in_specs=[vmem_spec()] * len(operands),
        out_specs=[vmem_spec()] * len(out_shape) if many else vmem_spec(),
        scratch_shapes=list(scratch),
        compiler_params=pltpu.CompilerParams(vmem_limit_bytes=limit * MIB),
    )(*operands)


def first_lift(own, partner, lifters):
    leaves, rank, columns = own.shape
    half = columns // 2

    def body(own_ref, partner_ref, lifter_ref, out_ref):
        low = lax.axis_index("gz") & 1
        total = None
        cols = pl.ds(pl.multiple_of(low * half, half), half)
        for source, place in ((own_ref, low), (partner_ref, 1 - low)):
            for leaf in range(leaves):
                first = pl.multiple_of((place * leaves + leaf) * rank, rank)
                term = dot_t(lifter_ref[0, 0, pl.ds(first, rank), :], source[leaf, :, cols])
                total = term if total is None else total + term
        out_ref[...] = total.astype(jnp.bfloat16)

    return call_small(
        body, "first_lift", pltpu.VMEM((rank, half), jnp.bfloat16), [own, partner, lifters]
    )


def next_lift(own, others, lifters, stage, axis, shift, after):
    rank, half = own.shape

    def body(own_ref, a_ref, b_ref, c_ref, lifter_ref, after_ref, out_ref):
        slot = slot_of(axis, shift)
        total = None
        for step, source in enumerate((own_ref, a_ref, b_ref, c_ref)):
            first = pl.multiple_of((slot ^ step) * rank, rank)
            term = dot_t(lifter_ref[0, stage + 1, pl.ds(first, rank), :], source[...])
            total = term if total is None else total + term
        out_ref[...] = total.astype(jnp.bfloat16)

    return call_small(
        body, "next_lift", pltpu.VMEM((rank, half), jnp.bfloat16), [own, *others, lifters, after]
    )


def far_sum(sources, coupling_ref, stage, slot):
    total = None
    for step, source in enumerate(sources, 1):
        _, place = sibling(slot, step)
        term = dot(coupling_ref[0, stage, place], source[...])
        total = term if total is None else total + term
    return total


def far_of(others, couplings, stage, axis, shift, after):
    rank, half = others[0].shape

    def body(a_ref, b_ref, c_ref, coupling_ref, after_ref, out_ref):
        out_ref[...] = far_sum(
            (a_ref, b_ref, c_ref), coupling_ref, stage, slot_of(axis, shift)
        )

    return call_small(
        body, "far_of", pltpu.VMEM((rank, half), jnp.float32), [*others, couplings, after]
    )


def go_down(others, fars, couplings, lowers, places):
    rank, half = others[0].shape
    top = len(places) - 1

    def body(*refs):
        a_ref, b_ref, c_ref, coupling_ref, lower_ref = refs[:5]
        far_refs = refs[5:-1]
        value = far_sum((a_ref, b_ref, c_ref), coupling_ref, top, slot_of(*places[top]))
        for stage in range(top - 1, -1, -1):
            first = pl.multiple_of(slot_of(*places[stage]) * rank, rank)
            block = lower_ref[0, stage + 1, pl.ds(first, rank), :]
            value = far_refs[stage][...] + dot(block, value.astype(jnp.bfloat16))
        refs[-1][...] = value.astype(jnp.bfloat16)

    return call_small(
        body,
        "go_down",
        pltpu.VMEM((rank, half), jnp.bfloat16),
        [*others, couplings, lowers, *fars],
    )


def local_part(
    rounded, ordered, own, partner, near, basis_out, leaf_coupling, lowers, order, ridge, after
):
    rows, columns = rounded.shape
    leaves, leaf_rows, _ = near.shape
    rank = basis_out.shape[2]
    tiles = columns // LANES
    rank_tiles = rank // LANES
    width = -(-(tiles + rank_tiles) // 8) * 8
    chunk = 256
    unroll = 16

    def body(
        order_hbm,
        ridge_ref,
        rounded_ref,
        ordered_ref,
        own_ref,
        partner_ref,
        near_ref,
        basis_ref,
        coupling_ref,
        lower_ref,
        after_ref,
        base_ref,
        spread_ref,
        children,
        tree,
        initial,
        order_ref,
        order_sem,
    ):
        low = lax.axis_index("gz") & 1
        order_copy = pltpu.make_async_copy(order_hbm, order_ref, order_sem)
        order_copy.start()
        children[pl.ds(low * leaves, leaves)] = own_ref[...]
        children[pl.ds((1 - low) * leaves, leaves)] = partner_ref[...]
        tree_flat = tree.reshape(rows * width, LANES)
        ordered_flat = ordered_ref.reshape(rows * tiles, LANES)
        initial_flat = initial.reshape(rows * width, LANES)
        ridge_value = ridge_ref[0]
        for leaf in range(leaves):
            slot = low * leaves + leaf
            far = None
            for t in range(ARITY - 1):
                source = t + (t >= slot).astype(jnp.int32)
                term = dot(coupling_ref[leaf, t], children[source])
                far = term if far is None else far + term
            far = far.astype(jnp.bfloat16)
            first = pl.multiple_of(slot * rank, rank)
            lower = lower_ref[0, 0, pl.ds(first, rank), :]
            values = rounded_ref[leaf * leaf_rows : (leaf + 1) * leaf_rows, :]

            def tile(block, _):
                inner = pl.multiple_of(block * chunk, chunk)
                outer = inner + leaf * leaf_rows
                basis = basis_ref[leaf, pl.ds(inner, chunk), :]
                value = dot(near_ref[leaf, pl.ds(inner, chunk), :], values) + dot(basis, far)
                for t in range(tiles):
                    kept = ordered_flat[pl.ds(outer * tiles + t, chunk, stride=tiles), :]
                    tree_flat[pl.ds(outer * width + t, chunk, stride=width), :] = (
                        value[:, t * LANES : (t + 1) * LANES] + ridge_value * kept
                    )
                span = dot(basis, lower)
                for t in range(rank_tiles):
                    tree_flat[pl.ds(outer * width + tiles + t, chunk, stride=width), :] = span[
                        :, t * LANES : (t + 1) * LANES
                    ]
                return 0

            lax.fori_loop(0, leaf_rows // chunk, tile, 0)
        order_copy.wait()

        def move(block, _):
            base = pl.multiple_of(block * unroll, unroll)
            for u in range(unroll):
                initial[local_row(order_ref[base + u], rows)] = tree[base + u]
            return 0

        lax.fori_loop(0, rows // unroll, move, 0)

        def spread(block, _):
            base = pl.multiple_of(block * chunk, chunk)
            for t in range(tiles):
                base_ref[pl.ds(base, chunk), t * LANES : (t + 1) * LANES] = initial_flat[
                    pl.ds(base * width + t, chunk, stride=width), :
                ]
            for t in range(rank_tiles):
                spread_ref[pl.ds(base, chunk), t * LANES : (t + 1) * LANES] = initial_flat[
                    pl.ds(base * width + tiles + t, chunk, stride=width), :
                ].astype(jnp.bfloat16)
            return 0

        lax.fori_loop(0, rows // chunk, spread, 0)

    hbm_spec = pl.BlockSpec(memory_space=pltpu.HBM)
    smem_spec = pl.BlockSpec(memory_space=pltpu.SMEM)
    return pl.pallas_call(
        body,
        name="local_part",
        out_shape=[
            pltpu.VMEM((rows, columns), jnp.float32),
            pltpu.VMEM((rows, rank), jnp.bfloat16),
        ],
        in_specs=[hbm_spec, smem_spec] + [vmem_spec()] * 9,
        out_specs=[vmem_spec()] * 2,
        scratch_shapes=[
            pltpu.VMEM((ARITY, rank, columns), jnp.bfloat16),
            pltpu.VMEM((rows, width, LANES), jnp.float32),
            pltpu.VMEM((rows, width, LANES), jnp.float32),
            pltpu.SMEM(order.shape, order.dtype),
            pltpu.SemaphoreType.DMA,
        ],
        compiler_params=pltpu.CompilerParams(vmem_limit_bytes=20 * MIB),
    )(
        stay(order),
        ridge,
        rounded,
        ordered,
        own,
        partner,
        near,
        basis_out,
        leaf_coupling,
        lowers,
        after,
    )


def finish(base, spread, own, partner):
    rows, columns = base.shape
    rank, half = own.shape
    parts = 8
    step = rows // parts

    def body(base_ref, spread_ref, own_ref, partner_ref, out_ref, low_ref, result, sems):
        low = lax.axis_index("gz") & 1
        low_ref[:, pl.ds(pl.multiple_of(low * half, half), half)] = own_ref[...]
        low_ref[:, pl.ds(pl.multiple_of((1 - low) * half, half), half)] = partner_ref[...]
        copies = []
        for p in range(parts):
            piece = slice(p * step, (p + 1) * step)
            result[piece, :] = base_ref[piece, :] + dot(spread_ref[piece, :], low_ref[...])
            copy = pltpu.make_async_copy(
                result.at[pl.ds(p * step, step), :],
                out_ref.at[pl.ds(p * step, step), :],
                sems.at[p],
            )
            copy.start()
            copies.append(copy)
        for copy in copies:
            copy.wait()

    return pl.pallas_call(
        body,
        name="finish",
        out_shape=jax.ShapeDtypeStruct((rows, columns), jnp.float32),
        in_specs=[vmem_spec()] * 4,
        out_specs=pl.BlockSpec(memory_space=pl.ANY),
        scratch_shapes=[
            pltpu.VMEM((rank, columns), jnp.bfloat16),
            pltpu.VMEM((rows, columns), jnp.float32),
            pltpu.SemaphoreType.DMA((parts,)),
        ],
        compiler_params=pltpu.CompilerParams(vmem_limit_bytes=6 * MIB),
    )(base, spread, own, partner)


def swap(value, axis, mask):
    size = lax.axis_size(axis)
    return lax.ppermute(value, axis, [(s, s ^ mask) for s in range(size)])


def on_device(
    points,
    order,
    near,
    basis_in,
    basis_out,
    leaf_coupling,
    transfer_up,
    transfer_down,
    node_coupling,
    ridge,
):
    stages = transfer_up.shape[1]
    places = [("gz", 1 + 2 * i) for i in range(stages - 2)] + [("gy", 0), ("gx", 0)]
    held = [transfer_up, node_coupling, transfer_down, leaf_coupling, basis_out, near]
    rounded, leaf_hat, ordered, *kept = upward_leaves(points, order, basis_in, held)
    lifters, couplings, lowers, leaf_couplings, bases, blocks = kept
    partner_hat = swap(leaf_hat, "gz", 1)
    hat = first_lift(leaf_hat, partner_hat, lifters)
    base = spread = None
    fars = []
    for stage, (axis, shift) in enumerate(places):
        others = [swap(hat, axis, step << shift) for step in (1, 2, 3)]
        if base is None:
            base, spread = local_part(
                rounded,
                ordered,
                leaf_hat,
                partner_hat,
                blocks,
                bases,
                leaf_couplings,
                lowers,
                order,
                ridge,
                hat,
            )
        if stage + 1 < stages:
            hat = next_lift(hat, others, lifters, stage, axis, shift, spread)
            fars.append(far_of(others, couplings, stage, axis, shift, hat))
    value = go_down(others, fars, couplings, lowers, places)
    partner_value = swap(value, "gz", 1)
    return finish(base, spread, value, partner_value)


def solution(mesh):
    placed = (
        P(("gx", "gy", "gz"), None),
        P(("gx", "gy", "gz")),
        P(("gx", "gy", "gz"), None, None),
        P(("gx", "gy", "gz"), None, None),
        P(("gx", "gy", "gz"), None, None),
        P(("gx", "gy", "gz"), None, None, None),
        P(("gx", "gy", "gz"), None, None, None),
        P(("gx", "gy", "gz"), None, None, None),
        P(("gx", "gy", "gz"), None, None, None, None),
        P(),
    )
    return jax.shard_map(
        on_device,
        mesh=mesh,
        in_specs=placed,
        out_specs=P(("gx", "gy", "gz"), None),
        check_vma=False,
    )
```

```python
import jax
import jax.numpy as jnp
from jax import lax
from jax.experimental import pallas as pl
from jax.experimental.pallas import tpu as pltpu
from jax.sharding import PartitionSpec as P

LANES = 128
ARITY = 4
MIB = 1 << 20


def vmem_spec():
    return pl.BlockSpec(memory_space=pltpu.VMEM)


def stay(value):
    return pltpu.with_memory_space_constraint(value, pltpu.HBM)


def dot(left, right):
    return jnp.dot(left, right, preferred_element_type=jnp.float32)


def dot_t(left, right):
    return lax.dot_general(
        left, right, (((0,), (0,)), ((), ())), preferred_element_type=jnp.float32
    )


def local_row(value, rows):
    if rows & (rows - 1) == 0:
        return value & (rows - 1)
    return lax.rem(value, rows)


def slot_of(axis, shift):
    return (lax.axis_index(axis) >> shift) & (ARITY - 1)


def sibling(slot, step):
    other = slot ^ step
    return other, other - (other > slot).astype(jnp.int32)


def upward_leaves(points, order, basis_in, held):
    rows, columns = points.shape
    leaves, leaf_rows, rank = basis_in.shape
    tiles = columns // LANES
    parts = 4
    step = rows // parts
    chunk = 256
    count = len(held)

    def body(*refs):
        order_hbm, points_ref, basis_hbm = refs[:3]
        held_in = refs[3 : 3 + count]
        rounded_ref, hat_ref, tiled, local_ref = refs[3 + count : 7 + count]
        held_out = refs[7 + count : 7 + 2 * count]
        plain, gathered, total, basis_ref, order_ref = refs[7 + 2 * count : 12 + 2 * count]
        sems, basis_sem, order_sems, held_sems = refs[12 + 2 * count :]
        order_copy = pltpu.make_async_copy(order_hbm, local_ref, order_sems.at[0])
        order_copy.start()
        copies = [
            pltpu.make_async_copy(
                points_ref.at[pl.ds(p * step, step), :],
                plain.at[pl.ds(p * step, step), :],
                sems.at[p],
            )
            for p in range(parts)
        ]
        for copy in copies:
            copy.start()
        basis_copy = pltpu.make_async_copy(basis_hbm, basis_ref, basis_sem)
        basis_copy.start()
        held_copies = [
            pltpu.make_async_copy(src, dst, held_sems.at[i])
            for i, (src, dst) in enumerate(zip(held_in, held_out))
        ]
        order_copy.wait()
        local_ref[...] = local_row(local_ref[...], rows)
        local_copy = pltpu.make_async_copy(local_ref, order_ref, order_sems.at[1])
        local_copy.start()
        tiled_flat = tiled.reshape(rows * tiles, LANES)
        gathered_flat = gathered.reshape(rows * tiles, LANES)
        for p, copy in enumerate(copies):
            copy.wait()
            for t in range(tiles):
                tiled_flat[pl.ds(p * step * tiles + t, step, stride=tiles), :] = plain[
                    p * step : (p + 1) * step, t * LANES : (t + 1) * LANES
                ]
        for copy in held_copies:
            copy.start()
        local_copy.wait()
        basis_copy.wait()

        def take(block):
            for i in range(block * chunk, (block + 1) * chunk):
                gathered[i] = tiled[order_ref[i]]

        def use(block):
            outer = block * chunk
            leaf = outer // leaf_rows
            inner = outer - leaf * leaf_rows
            for t in range(tiles):
                rounded_ref[outer : outer + chunk, t * LANES : (t + 1) * LANES] = gathered_flat[
                    pl.ds(outer * tiles + t, chunk, stride=tiles), :
                ].astype(jnp.bfloat16)
            term = dot_t(
                basis_ref[leaf, inner : inner + chunk, :], rounded_ref[outer : outer + chunk, :]
            )
            if inner > 0:
                term = term + total[...]
            if inner + chunk == leaf_rows:
                hat_ref[leaf] = term.astype(jnp.bfloat16)
            else:
                total[...] = term

        blocks = rows // chunk
        for block in range(blocks):
            if block:
                use(block - 1)
            take(block)
        use(blocks - 1)
        for copy in held_copies:
            copy.wait()

    hbm_spec = pl.BlockSpec(memory_space=pltpu.HBM)
    return pl.pallas_call(
        body,
        name="upward_leaves",
        out_shape=[
            pltpu.VMEM((rows, columns), jnp.bfloat16),
            pltpu.VMEM((leaves, rank, columns), jnp.bfloat16),
            pltpu.VMEM((rows, tiles, LANES), jnp.float32),
            pltpu.VMEM(order.shape, order.dtype),
        ]
        + [pltpu.VMEM(h.shape, h.dtype) for h in held],
        in_specs=[hbm_spec] * (3 + count),
        out_specs=[vmem_spec()] * (4 + count),
        scratch_shapes=[
            pltpu.VMEM((rows, columns), jnp.float32),
            pltpu.VMEM((rows, tiles, LANES), jnp.float32),
            pltpu.VMEM((rank, columns), jnp.float32),
            pltpu.VMEM(basis_in.shape, basis_in.dtype),
            pltpu.SMEM(order.shape, order.dtype),
            pltpu.SemaphoreType.DMA((parts,)),
            pltpu.SemaphoreType.DMA,
            pltpu.SemaphoreType.DMA((2,)),
            pltpu.SemaphoreType.DMA((count,)),
        ],
        compiler_params=pltpu.CompilerParams(vmem_limit_bytes=14 * MIB),
    )(*[stay(value) for value in (order, points, basis_in, *held)])


def call_small(body, name, out_shape, operands, scratch=(), limit=4):
    many = isinstance(out_shape, list)
    return pl.pallas_call(
        body,
        name=name,
        out_shape=out_shape,
        in_specs=[vmem_spec()] * len(operands),
        out_specs=[vmem_spec()] * len(out_shape) if many else vmem_spec(),
        scratch_shapes=list(scratch),
        compiler_params=pltpu.CompilerParams(vmem_limit_bytes=limit * MIB),
    )(*operands)


def first_lift(own, partner, lifters):
    leaves, rank, columns = own.shape
    half = columns // 2

    def body(own_ref, partner_ref, lifter_ref, out_ref):
        low = lax.axis_index("gz") & 1
        total = None
        cols = pl.ds(pl.multiple_of(low * half, half), half)
        for source, place in ((own_ref, low), (partner_ref, 1 - low)):
            for leaf in range(leaves):
                first = pl.multiple_of((place * leaves + leaf) * rank, rank)
                term = dot_t(lifter_ref[0, 0, pl.ds(first, rank), :], source[leaf, :, cols])
                total = term if total is None else total + term
        out_ref[...] = total.astype(jnp.bfloat16)

    return call_small(
        body, "first_lift", pltpu.VMEM((rank, half), jnp.bfloat16), [own, partner, lifters]
    )


def next_lift(own, others, lifters, stage, axis, shift, after):
    rank, half = own.shape

    def body(own_ref, a_ref, b_ref, c_ref, lifter_ref, after_ref, out_ref):
        slot = slot_of(axis, shift)
        total = None
        for step, source in enumerate((own_ref, a_ref, b_ref, c_ref)):
            first = pl.multiple_of((slot ^ step) * rank, rank)
            term = dot_t(lifter_ref[0, stage + 1, pl.ds(first, rank), :], source[...])
            total = term if total is None else total + term
        out_ref[...] = total.astype(jnp.bfloat16)

    return call_small(
        body, "next_lift", pltpu.VMEM((rank, half), jnp.bfloat16), [own, *others, lifters, after]
    )


def far_sum(sources, coupling_ref, stage, slot):
    total = None
    for step, source in enumerate(sources, 1):
        _, place = sibling(slot, step)
        term = dot(coupling_ref[0, stage, place], source[...])
        total = term if total is None else total + term
    return total


def far_of(others, couplings, stage, axis, shift, after):
    rank, half = others[0].shape

    def body(a_ref, b_ref, c_ref, coupling_ref, after_ref, out_ref):
        out_ref[...] = far_sum(
            (a_ref, b_ref, c_ref), coupling_ref, stage, slot_of(axis, shift)
        )

    return call_small(
        body, "far_of", pltpu.VMEM((rank, half), jnp.float32), [*others, couplings, after]
    )


def go_down(others, fars, couplings, lowers, places, after):
    rank, half = others[0].shape
    top = len(places) - 1

    def body(*refs):
        a_ref, b_ref, c_ref, coupling_ref, lower_ref = refs[:5]
        far_refs = refs[5:-2]
        value = far_sum((a_ref, b_ref, c_ref), coupling_ref, top, slot_of(*places[top]))
        for stage in range(top - 1, -1, -1):
            first = pl.multiple_of(slot_of(*places[stage]) * rank, rank)
            block = lower_ref[0, stage + 1, pl.ds(first, rank), :]
            value = far_refs[stage][...] + dot(block, value.astype(jnp.bfloat16))
        refs[-1][...] = value.astype(jnp.bfloat16)

    return call_small(
        body,
        "go_down",
        pltpu.VMEM((rank, half), jnp.bfloat16),
        [*others, couplings, lowers, *fars, after],
    )


def tree_part(rounded, own, partner, near, basis_out, leaf_coupling, lowers, after):
    rows, columns = rounded.shape
    leaves, leaf_rows, _ = near.shape
    rank = basis_out.shape[2]
    tiles = columns // LANES
    rank_tiles = rank // LANES
    width = -(-(tiles + rank_tiles) // 8) * 8
    chunk = 256
    per_leaf = leaf_rows // chunk

    def body(
        near_hbm,
        rounded_ref,
        own_ref,
        partner_ref,
        basis_ref,
        coupling_ref,
        lower_ref,
        after_ref,
        tree,
        near_ref,
        children,
        sems,
    ):
        low = lax.axis_index("gz") & 1
        copies = []
        for leaf in range(leaves):
            for block in range(per_leaf):
                copies.append(
                    pltpu.make_async_copy(
                        near_hbm.at[leaf, pl.ds(block * chunk, chunk), :],
                        near_ref.at[leaf, pl.ds(block * chunk, chunk), :],
                        sems.at[leaf * per_leaf + block],
                    )
                )
                copies[-1].start()
        children[pl.ds(low * leaves, leaves)] = own_ref[...]
        children[pl.ds((1 - low) * leaves, leaves)] = partner_ref[...]
        tree_flat = tree.reshape(rows * width, LANES)
        fars = []
        for leaf in range(leaves):
            slot = low * leaves + leaf
            far = None
            for t in range(ARITY - 1):
                source = t + (t >= slot).astype(jnp.int32)
                term = dot(coupling_ref[leaf, t], children[source])
                far = term if far is None else far + term
            fars.append(far.astype(jnp.bfloat16))
            lower = lower_ref[0, 0, pl.ds(pl.multiple_of(slot * rank, rank), rank), :]
            span = dot(basis_ref[leaf], lower)
            for t in range(rank_tiles):
                first = leaf * leaf_rows * width + tiles + t
                tree_flat[pl.ds(first, leaf_rows, stride=width), :] = span[
                    :, t * LANES : (t + 1) * LANES
                ]
        for leaf in range(leaves):
            values = rounded_ref[leaf * leaf_rows : (leaf + 1) * leaf_rows, :]
            for block in range(per_leaf):
                copies[leaf * per_leaf + block].wait()
                piece = slice(block * chunk, (block + 1) * chunk)
                value = dot(near_ref[leaf, piece, :], values)
                value = value + dot(basis_ref[leaf, piece, :], fars[leaf])
                for t in range(tiles):
                    first = (leaf * leaf_rows + block * chunk) * width + t
                    tree_flat[pl.ds(first, chunk, stride=width), :] = value[
                        :, t * LANES : (t + 1) * LANES
                    ]

    hbm_spec = pl.BlockSpec(memory_space=pltpu.HBM)
    return pl.pallas_call(
        body,
        name="tree_part",
        out_shape=pltpu.VMEM((rows, width, LANES), jnp.float32),
        in_specs=[hbm_spec] + [vmem_spec()] * 7,
        out_specs=vmem_spec(),
        scratch_shapes=[
            pltpu.VMEM(near.shape, near.dtype),
            pltpu.VMEM((ARITY, rank, columns), jnp.bfloat16),
            pltpu.SemaphoreType.DMA((leaves * per_leaf,)),
        ],
        compiler_params=pltpu.CompilerParams(vmem_limit_bytes=10 * MIB),
    )(stay(near), rounded, own, partner, basis_out, leaf_coupling, lowers, after)


def to_initial(tree, tiled, local, ridge, rank, after):
    rows, width, _ = tree.shape
    tiles = tiled.shape[1]
    rank_tiles = rank // LANES
    chunk = 256

    def body(
        ridge_ref, tree_ref, tiled_ref, local_ref, after_ref, base_ref, spread_ref, initial, order_ref, sem
    ):
        copy = pltpu.make_async_copy(local_ref, order_ref, sem)
        copy.start()
        ridge_value = ridge_ref[0]
        initial_flat = initial.reshape(rows * width, LANES)
        tiled_flat = tiled_ref.reshape(rows * tiles, LANES)
        copy.wait()
        for i in range(rows):
            initial[order_ref[i]] = tree_ref[i]

        def spread(block, _):
            base = pl.multiple_of(block * chunk, chunk)
            for t in range(tiles):
                kept = tiled_flat[pl.ds(base * tiles + t, chunk, stride=tiles), :]
                base_ref[pl.ds(base, chunk), t * LANES : (t + 1) * LANES] = (
                    initial_flat[pl.ds(base * width + t, chunk, stride=width), :]
                    + ridge_value * kept
                )
            for t in range(rank_tiles):
                spread_ref[pl.ds(base, chunk), t * LANES : (t + 1) * LANES] = initial_flat[
                    pl.ds(base * width + tiles + t, chunk, stride=width), :
                ].astype(jnp.bfloat16)
            return 0

        lax.fori_loop(0, rows // chunk, spread, 0)

    smem_spec = pl.BlockSpec(memory_space=pltpu.SMEM)
    return pl.pallas_call(
        body,
        name="to_initial",
        out_shape=[
            pltpu.VMEM((rows, tiles * LANES), jnp.float32),
            pltpu.VMEM((rows, rank), jnp.bfloat16),
        ],
        in_specs=[smem_spec] + [vmem_spec()] * 4,
        out_specs=[vmem_spec()] * 2,
        scratch_shapes=[
            pltpu.VMEM((rows, width, LANES), jnp.float32),
            pltpu.SMEM(local.shape, local.dtype),
            pltpu.SemaphoreType.DMA,
        ],
        compiler_params=pltpu.CompilerParams(vmem_limit_bytes=10 * MIB),
    )(ridge, tree, tiled, local, after)


def finish(base, spread, own, partner):
    rows, columns = base.shape
    rank, half = own.shape
    parts = 8
    step = rows // parts

    def body(base_ref, spread_ref, own_ref, partner_ref, out_ref, low_ref, result, sems):
        low = lax.axis_index("gz") & 1
        low_ref[:, pl.ds(pl.multiple_of(low * half, half), half)] = own_ref[...]
        low_ref[:, pl.ds(pl.multiple_of((1 - low) * half, half), half)] = partner_ref[...]
        copies = []
        for p in range(parts):
            piece = slice(p * step, (p + 1) * step)
            result[piece, :] = base_ref[piece, :] + dot(spread_ref[piece, :], low_ref[...])
            copy = pltpu.make_async_copy(
                result.at[pl.ds(p * step, step), :],
                out_ref.at[pl.ds(p * step, step), :],
                sems.at[p],
            )
            copy.start()
            copies.append(copy)
        for copy in copies:
            copy.wait()

    return pl.pallas_call(
        body,
        name="finish",
        out_shape=jax.ShapeDtypeStruct((rows, columns), jnp.float32),
        in_specs=[vmem_spec()] * 4,
        out_specs=pl.BlockSpec(memory_space=pl.ANY),
        scratch_shapes=[
            pltpu.VMEM((rank, columns), jnp.bfloat16),
            pltpu.VMEM((rows, columns), jnp.float32),
            pltpu.SemaphoreType.DMA((parts,)),
        ],
        compiler_params=pltpu.CompilerParams(vmem_limit_bytes=6 * MIB),
    )(base, spread, own, partner)


def swap(value, axis, mask):
    size = lax.axis_size(axis)
    return lax.ppermute(value, axis, [(s, s ^ mask) for s in range(size)])


def on_device(
    points,
    order,
    near,
    basis_in,
    basis_out,
    leaf_coupling,
    transfer_up,
    transfer_down,
    node_coupling,
    ridge,
):
    stages = transfer_up.shape[1]
    places = [("gz", 1 + 2 * i) for i in range(stages - 2)] + [("gy", 0), ("gx", 0)]
    held = [transfer_up, leaf_coupling, basis_out, transfer_down, node_coupling]
    rounded, leaf_hat, tiled, local, *kept = upward_leaves(points, order, basis_in, held)
    lifters, leaf_couplings, bases, lowers, couplings = kept
    partner_hat = swap(leaf_hat, "gz", 1)
    hat = first_lift(leaf_hat, partner_hat, lifters)
    tree = tree_part(
        rounded, leaf_hat, partner_hat, near, bases, leaf_couplings, lowers, hat
    )
    fars = []
    rank = basis_in.shape[2]
    for stage, (axis, shift) in enumerate(places):
        others = [swap(hat, axis, step << shift) for step in (1, 2, 3)]
        if stage == 1:
            base, spread = to_initial(tree, tiled, local, ridge, rank, hat)
        if stage + 1 < stages:
            hat = next_lift(hat, others, lifters, stage, axis, shift, tree if stage == 0 else hat)
            fars.append(far_of(others, couplings, stage, axis, shift, hat))
    value = go_down(others, fars, couplings, lowers, places, spread)
    partner_value = swap(value, "gz", 1)
    return finish(base, spread, value, partner_value)


def solution(mesh):
    placed = (
        P(("gx", "gy", "gz"), None),
        P(("gx", "gy", "gz")),
        P(("gx", "gy", "gz"), None, None),
        P(("gx", "gy", "gz"), None, None),
        P(("gx", "gy", "gz"), None, None),
        P(("gx", "gy", "gz"), None, None, None),
        P(("gx", "gy", "gz"), None, None, None),
        P(("gx", "gy", "gz"), None, None, None),
        P(("gx", "gy", "gz"), None, None, None, None),
        P(),
    )
    return jax.shard_map(
        on_device,
        mesh=mesh,
        in_specs=placed,
        out_specs=P(("gx", "gy", "gz"), None),
        check_vma=False,
    )
```

```python
import jax
import jax.numpy as jnp
from jax import lax
from jax.experimental import pallas as pl
from jax.experimental.pallas import tpu as pltpu
from jax.sharding import PartitionSpec as P


LANES = 128
ARITY = 4
MIB = 1 << 20
LEAD = 32


def vmem_spec():
    return pl.BlockSpec(memory_space=pltpu.VMEM)


def stay(value):
    return pltpu.with_memory_space_constraint(value, pltpu.HBM)


def dot(left, right):
    return jnp.dot(left, right, preferred_element_type=jnp.float32)


def dot_t(left, right):
    return lax.dot_general(
        left, right, (((0,), (0,)), ((), ())), preferred_element_type=jnp.float32
    )


def local_row(value, rows):
    if rows & (rows - 1) == 0:
        return value & (rows - 1)
    return lax.rem(value, rows)


def slot_of(axis, shift):
    return (lax.axis_index(axis) >> shift) & (ARITY - 1)


def sibling(slot, step):
    other = slot ^ step
    return other, other - (other > slot).astype(jnp.int32)


def upward_leaves(points, order, basis_in, held):
    rows, columns = points.shape
    leaves, leaf_rows, rank = basis_in.shape
    tiles = columns // LANES
    half = columns // 2
    parts = 4
    step = rows // parts
    chunk = 256
    per_leaf = leaf_rows // chunk
    blocks = rows // chunk
    count = len(held)

    def body(*refs):
        order_hbm, points_ref, basis_hbm = refs[:3]
        held_in = refs[3 : 3 + count]
        rounded_ref, hat_ref, tiled, local_ref, kept_ref, sent_ref = refs[3 + count : 9 + count]
        held_out = refs[9 + count : 9 + 2 * count]
        plain, gathered, total, basis_ref, order_ref = refs[9 + 2 * count : 14 + 2 * count]
        sems, basis_sem, order_sems, held_sems = refs[14 + 2 * count :]
        order_copy = pltpu.make_async_copy(order_hbm, local_ref, order_sems.at[0])
        order_copy.start()
        copies = [
            pltpu.make_async_copy(
                points_ref.at[pl.ds(p * step, step), :],
                plain.at[pl.ds(p * step, step), :],
                sems.at[p],
            )
            for p in range(parts)
        ]
        for copy in copies:
            copy.start()
        basis_copy = pltpu.make_async_copy(basis_hbm, basis_ref, basis_sem)
        basis_copy.start()
        held_copies = [
            pltpu.make_async_copy(src, dst, held_sems.at[i])
            for i, (src, dst) in enumerate(zip(held_in, held_out))
        ]
        total[...] = jnp.zeros(total.shape, total.dtype)
        order_copy.wait()
        local_ref[...] = local_row(local_ref[...], rows)
        local_copy = pltpu.make_async_copy(local_ref, order_ref, order_sems.at[1])
        local_copy.start()
        tiled_flat = tiled.reshape(rows * tiles, LANES)
        gathered_flat = gathered.reshape(rows * tiles, LANES)
        for p, copy in enumerate(copies):
            copy.wait()
            for t in range(tiles):
                tiled_flat[pl.ds(p * step * tiles + t, step, stride=tiles), :] = plain[
                    p * step : (p + 1) * step, t * LANES : (t + 1) * LANES
                ]
        for copy in held_copies:
            copy.start()
        local_copy.wait()
        basis_copy.wait()

        def take(first, size):
            for u in range(size):
                gathered[first + u] = tiled[order_ref[first + u]]

        def use(block):
            outer = pl.multiple_of(block * chunk, chunk)
            leaf = block // per_leaf
            inner = pl.multiple_of((block - leaf * per_leaf) * chunk, chunk)
            for t in range(tiles):
                rounded_ref[pl.ds(outer, chunk), t * LANES : (t + 1) * LANES] = gathered_flat[
                    pl.ds(outer * tiles + t, chunk, stride=tiles), :
                ].astype(jnp.bfloat16)
            total[leaf] += dot_t(
                basis_ref[leaf, pl.ds(inner, chunk), :], rounded_ref[pl.ds(outer, chunk), :]
            )

        def lead(piece, _):
            take(pl.multiple_of(piece * LEAD, LEAD), LEAD)
            return 0

        def both(block, _):
            use(block - 1)
            take(pl.multiple_of(block * chunk, chunk), chunk)
            return 0

        lax.fori_loop(0, chunk // LEAD, lead, 0)
        lax.fori_loop(1, blocks, both, 0)
        use(jnp.int32(blocks - 1))
        low = lax.axis_index("gz") & 1
        held_copies[0].wait()
        for place, target in ((low, kept_ref), (1 - low, sent_ref)):
            cols = pl.ds(pl.multiple_of(place * half, half), half)
            value = None
            for leaf in range(leaves):
                piece = total[leaf, :, cols].astype(jnp.bfloat16)
                hat_ref[leaf, :, cols] = piece
                first = pl.multiple_of((low * leaves + leaf) * rank, rank)
                term = dot_t(held_out[0][0, 0, pl.ds(first, rank), :], piece)
                value = term if value is None else value + term
            target[...] = value.astype(target.dtype)
        for copy in held_copies[1:]:
            copy.wait()

    hbm_spec = pl.BlockSpec(memory_space=pltpu.HBM)
    return pl.pallas_call(
        body,
        name="upward_leaves",
        out_shape=[
            pltpu.VMEM((rows, columns), jnp.bfloat16),
            pltpu.VMEM((leaves, rank, columns), jnp.bfloat16),
            pltpu.VMEM((rows, tiles, LANES), jnp.float32),
            pltpu.VMEM(order.shape, order.dtype),
            pltpu.VMEM((rank, half), jnp.float32),
            pltpu.VMEM((rank, half), jnp.bfloat16),
        ]
        + [pltpu.VMEM(h.shape, h.dtype) for h in held],
        in_specs=[hbm_spec] * (3 + count),
        out_specs=[vmem_spec()] * (6 + count),
        scratch_shapes=[
            pltpu.VMEM((rows, columns), jnp.float32),
            pltpu.VMEM((rows, tiles, LANES), jnp.float32),
            pltpu.VMEM((leaves, rank, columns), jnp.float32),
            pltpu.VMEM(basis_in.shape, basis_in.dtype),
            pltpu.SMEM(order.shape, order.dtype),
            pltpu.SemaphoreType.DMA((parts,)),
            pltpu.SemaphoreType.DMA,
            pltpu.SemaphoreType.DMA((2,)),
            pltpu.SemaphoreType.DMA((count,)),
        ],
        compiler_params=pltpu.CompilerParams(vmem_limit_bytes=14 * MIB),
    )(*[stay(value) for value in (order, points, basis_in, *held)])


def call_small(body, out_shape, operands, scratch=(), limit=4):
    many = isinstance(out_shape, list)
    return pl.pallas_call(
        body,
        out_shape=out_shape,
        in_specs=[vmem_spec()] * len(operands),
        out_specs=[vmem_spec()] * len(out_shape) if many else vmem_spec(),
        scratch_shapes=list(scratch),
        compiler_params=pltpu.CompilerParams(vmem_limit_bytes=limit * MIB),
    )(*operands)


def first_sum(kept, arrived):
    def body(kept_ref, arrived_ref, out_ref):
        out_ref[...] = (kept_ref[...] + arrived_ref[...].astype(jnp.float32)).astype(jnp.bfloat16)

    return call_small(body, pltpu.VMEM(arrived.shape, jnp.bfloat16), [kept, arrived])


def next_lift(own, others, lifters, stage, axis, shift, after):
    rank, half = own.shape

    def body(own_ref, a_ref, b_ref, c_ref, lifter_ref, after_ref, out_ref):
        slot = slot_of(axis, shift)
        total = None
        for step, source in enumerate((own_ref, a_ref, b_ref, c_ref)):
            first = pl.multiple_of((slot ^ step) * rank, rank)
            term = dot_t(lifter_ref[0, stage + 1, pl.ds(first, rank), :], source[...])
            total = term if total is None else total + term
        out_ref[...] = total.astype(jnp.bfloat16)

    return call_small(body, pltpu.VMEM((rank, half), jnp.bfloat16), [own, *others, lifters, after])


def far_sum(sources, coupling_ref, stage, slot):
    total = None
    for step, source in enumerate(sources, 1):
        _, place = sibling(slot, step)
        term = dot(coupling_ref[0, stage, place], source[...])
        total = term if total is None else total + term
    return total


def far_of(others, couplings, stage, axis, shift, after):
    rank, half = others[0].shape

    def body(a_ref, b_ref, c_ref, coupling_ref, after_ref, out_ref):
        out_ref[...] = far_sum(
            (a_ref, b_ref, c_ref), coupling_ref, stage, slot_of(axis, shift)
        )

    return call_small(body, pltpu.VMEM((rank, half), jnp.float32), [*others, couplings, after])


def go_down(others, fars, couplings, lowers, places, after):
    rank, half = others[0].shape
    top = len(places) - 1

    def body(*refs):
        a_ref, b_ref, c_ref, coupling_ref, lower_ref = refs[:5]
        far_refs = refs[5:-2]
        value = far_sum((a_ref, b_ref, c_ref), coupling_ref, top, slot_of(*places[top]))
        for stage in range(top - 1, -1, -1):
            first = pl.multiple_of(slot_of(*places[stage]) * rank, rank)
            block = lower_ref[0, stage + 1, pl.ds(first, rank), :]
            value = far_refs[stage][...] + dot(block, value.astype(jnp.bfloat16))
        refs[-1][...] = value.astype(jnp.bfloat16)

    return call_small(
        body, pltpu.VMEM((rank, half), jnp.bfloat16), [*others, couplings, lowers, *fars, after]
    )


def local_part(rounded, own, partner, near, basis_out, leaf_coupling, lowers, local, after):
    rows, columns = rounded.shape
    leaves, leaf_rows, _ = near.shape
    rank = basis_out.shape[2]
    tiles = columns // LANES
    rank_tiles = rank // LANES
    width = -(-(tiles + rank_tiles) // 8) * 8
    chunk = 256
    per_leaf = leaf_rows // chunk
    blocks = rows // chunk

    def body(
        near_hbm,
        rounded_ref,
        own_ref,
        partner_ref,
        basis_ref,
        coupling_ref,
        lower_ref,
        local_ref,
        after_ref,
        initial,
        tree,
        near_ref,
        children,
        fars,
        order_ref,
        sems,
        order_sem,
    ):
        low = lax.axis_index("gz") & 1
        order_copy = pltpu.make_async_copy(local_ref, order_ref, order_sem)
        order_copy.start()

        def near_copy(block):
            leaf = block // per_leaf
            piece = pl.ds(pl.multiple_of((block - leaf * per_leaf) * chunk, chunk), chunk)
            return pltpu.make_async_copy(
                near_hbm.at[leaf, piece, :], near_ref.at[leaf, piece, :], sems.at[block]
            )

        for block in range(blocks):
            near_copy(block).start()
        children[pl.ds(low * leaves, leaves)] = own_ref[...]
        children[pl.ds((1 - low) * leaves, leaves)] = partner_ref[...]
        tree_flat = tree.reshape(rows * width, LANES)
        for leaf in range(leaves):
            slot = low * leaves + leaf
            far = None
            for t in range(ARITY - 1):
                source = t + (t >= slot).astype(jnp.int32)
                term = dot(coupling_ref[leaf, t], children[source])
                far = term if far is None else far + term
            fars[leaf] = far.astype(jnp.bfloat16)
        order_copy.wait()

        def compute(block):
            leaf = block // per_leaf
            inner = pl.multiple_of((block - leaf * per_leaf) * chunk, chunk)
            outer = pl.multiple_of(block * chunk, chunk)
            near_copy(block).wait()
            basis = basis_ref[leaf, pl.ds(inner, chunk), :]
            values = rounded_ref[pl.ds(pl.multiple_of(leaf * leaf_rows, leaf_rows), leaf_rows), :]
            value = dot(near_ref[leaf, pl.ds(inner, chunk), :], values) + dot(basis, fars[leaf])
            first = pl.multiple_of((low * leaves + leaf) * rank, rank)
            span = dot(basis, lower_ref[0, 0, pl.ds(first, rank), :])
            for t in range(tiles):
                tree_flat[pl.ds(outer * width + t, chunk, stride=width), :] = value[
                    :, t * LANES : (t + 1) * LANES
                ]
            for t in range(rank_tiles):
                tree_flat[pl.ds(outer * width + tiles + t, chunk, stride=width), :] = span[
                    :, t * LANES : (t + 1) * LANES
                ]

        def scatter(first, size):
            for u in range(size):
                initial[order_ref[first + u]] = tree[first + u]

        def both(block, _):
            scatter(pl.multiple_of((block - 1) * chunk, chunk), chunk)
            compute(block)
            return 0

        def last(piece, _):
            scatter(pl.multiple_of((blocks - 1) * chunk + piece * LEAD, LEAD), LEAD)
            return 0

        compute(jnp.int32(0))
        lax.fori_loop(1, blocks, both, 0)
        lax.fori_loop(0, chunk // LEAD, last, 0)

    hbm_spec = pl.BlockSpec(memory_space=pltpu.HBM)
    return pl.pallas_call(
        body,
        name="local_part",
        out_shape=pltpu.VMEM((rows, width, LANES), jnp.float32),
        in_specs=[hbm_spec] + [vmem_spec()] * 8,
        out_specs=vmem_spec(),
        scratch_shapes=[
            pltpu.VMEM((rows, width, LANES), jnp.float32),
            pltpu.VMEM(near.shape, near.dtype),
            pltpu.VMEM((ARITY, rank, columns), jnp.bfloat16),
            pltpu.VMEM((leaves, rank, columns), jnp.bfloat16),
            pltpu.SMEM(local.shape, local.dtype),
            pltpu.SemaphoreType.DMA((blocks,)),
            pltpu.SemaphoreType.DMA,
        ],
        compiler_params=pltpu.CompilerParams(vmem_limit_bytes=16 * MIB),
    )(stay(near), rounded, own, partner, basis_out, leaf_coupling, lowers, local, after)


def to_rows(initial, tiled, ridge, rank, after):
    rows, width, _ = initial.shape
    tiles = tiled.shape[1]
    rank_tiles = rank // LANES
    chunk = 256

    def body(ridge_ref, initial_ref, tiled_ref, after_ref, base_ref, spread_ref):
        ridge_value = ridge_ref[0]
        initial_flat = initial_ref.reshape(rows * width, LANES)
        tiled_flat = tiled_ref.reshape(rows * tiles, LANES)

        def spread(block, _):
            base = pl.multiple_of(block * chunk, chunk)
            for t in range(tiles):
                kept = tiled_flat[pl.ds(base * tiles + t, chunk, stride=tiles), :]
                base_ref[pl.ds(base, chunk), t * LANES : (t + 1) * LANES] = (
                    initial_flat[pl.ds(base * width + t, chunk, stride=width), :]
                    + ridge_value * kept
                )
            for t in range(rank_tiles):
                spread_ref[pl.ds(base, chunk), t * LANES : (t + 1) * LANES] = initial_flat[
                    pl.ds(base * width + tiles + t, chunk, stride=width), :
                ].astype(jnp.bfloat16)
            return 0

        lax.fori_loop(0, rows // chunk, spread, 0)

    smem_spec = pl.BlockSpec(memory_space=pltpu.SMEM)
    return pl.pallas_call(
        body,
        name="to_rows",
        out_shape=[
            pltpu.VMEM((rows, tiles * LANES), jnp.float32),
            pltpu.VMEM((rows, rank), jnp.bfloat16),
        ],
        in_specs=[smem_spec] + [vmem_spec()] * 3,
        out_specs=[vmem_spec()] * 2,
        compiler_params=pltpu.CompilerParams(vmem_limit_bytes=4 * MIB),
    )(ridge, initial, tiled, after)


def finish(base, spread, lowered, other, previous):
    rows, columns = base.shape
    half = columns // 2
    parts = 4
    step = rows // parts

    def body(*refs):
        base_ref, spread_ref, lowered_ref = refs[:3]
        out_ref, result, sems = refs[-3:]
        place = lax.axis_index("gz") & 1
        if other:
            place = 1 - place
        cols = pl.ds(pl.multiple_of(place * half, half), half)
        copies = []
        for p in range(parts):
            piece = slice(p * step, (p + 1) * step)
            result[piece, :] = base_ref[piece, cols] + dot(spread_ref[piece, :], lowered_ref[...])
            copy = pltpu.make_async_copy(
                result.at[pl.ds(p * step, step), :],
                out_ref.at[pl.ds(p * step, step), cols],
                sems.at[p],
            )
            copy.start()
            copies.append(copy)
        for copy in copies:
            copy.wait()

    hbm_spec = pl.BlockSpec(memory_space=pltpu.HBM)
    extra = [] if previous is None else [previous]
    return pl.pallas_call(
        body,
        name="finish_other" if other else "finish_own",
        out_shape=pltpu.HBM((rows, columns), jnp.float32),
        in_specs=[vmem_spec()] * 3 + [hbm_spec] * len(extra),
        out_specs=hbm_spec,
        scratch_shapes=[
            pltpu.VMEM((rows, half), jnp.float32),
            pltpu.SemaphoreType.DMA((parts,)),
        ],
        input_output_aliases={3: 0} if extra else {},
        compiler_params=pltpu.CompilerParams(vmem_limit_bytes=4 * MIB),
    )(base, spread, lowered, *extra)


def swap(value, axis, mask):
    size = lax.axis_size(axis)
    return lax.ppermute(value, axis, [(s, s ^ mask) for s in range(size)])


def on_device(
    points,
    order,
    near,
    basis_in,
    basis_out,
    leaf_coupling,
    transfer_up,
    transfer_down,
    node_coupling,
    ridge,
):
    stages = transfer_up.shape[1]
    places = [("gz", 1 + 2 * i) for i in range(stages - 2)] + [("gy", 0), ("gx", 0)]
    held = [transfer_up, leaf_coupling, basis_out, transfer_down, node_coupling]
    rounded, leaf_hat, tiled, local, part, sent, *kept = upward_leaves(
        points, order, basis_in, held
    )
    lifters, leaf_couplings, bases, lowers, couplings = kept
    hat = first_sum(part, swap(sent, "gz", 1))
    fars = []
    rank = basis_in.shape[2]
    for stage, (axis, shift) in enumerate(places):
        others = []
        for step in (1, 2, 3):
            others.append(swap(hat, axis, step << shift))
        if stage == 0:
            leaf_hat, _ = lax.optimization_barrier((leaf_hat, hat))
            partner_hat = swap(leaf_hat, "gz", 1)
            initial = local_part(
                rounded, leaf_hat, partner_hat, near, bases, leaf_couplings, lowers, local, hat
            )
            after = initial
        if stage == 1:
            base, spread = to_rows(initial, tiled, ridge, rank, hat)
        if stage + 1 < stages:
            hat = next_lift(hat, others, lifters, stage, axis, shift, after)
            after = hat
            fars.append(far_of(others, couplings, stage, axis, shift, hat))
    value = go_down(others, fars, couplings, lowers, places, spread)
    partner_value = swap(value, "gz", 1)
    result = finish(base, spread, value, False, None)
    return finish(base, spread, partner_value, True, result)


def solution(mesh):
    placed = (
        P(("gx", "gy", "gz"), None),
        P(("gx", "gy", "gz")),
        P(("gx", "gy", "gz"), None, None),
        P(("gx", "gy", "gz"), None, None),
        P(("gx", "gy", "gz"), None, None),
        P(("gx", "gy", "gz"), None, None, None),
        P(("gx", "gy", "gz"), None, None, None),
        P(("gx", "gy", "gz"), None, None, None),
        P(("gx", "gy", "gz"), None, None, None, None),
        P(),
    )

    return jax.shard_map(
        on_device,
        mesh=mesh,
        in_specs=placed,
        out_specs=P(("gx", "gy", "gz"), None),
        check_vma=False,
    )
```

```python
import jax
import jax.numpy as jnp
from jax import lax
from jax.experimental import pallas as pl
from jax.experimental.pallas import tpu as pltpu
from jax.sharding import PartitionSpec as P


LANES = 128
ARITY = 4
STEPS = (2, 1, 3)
SUBLANES = 8
MIB = 1 << 20


def vmem_spec():
    return pl.BlockSpec(memory_space=pltpu.VMEM)


def stay(value):
    return pltpu.with_memory_space_constraint(value, pltpu.HBM)


def dot(left, right):
    return jnp.dot(left, right, preferred_element_type=jnp.float32)


def dot_t(left, right):
    return lax.dot_general(
        left, right, (((0,), (0,)), ((), ())), preferred_element_type=jnp.float32
    )


def local_row(value, rows):
    if rows & (rows - 1) == 0:
        return value & (rows - 1)
    return lax.rem(value, rows)


def slot_of(axis, shift):
    return (lax.axis_index(axis) >> shift) & (ARITY - 1)


def sibling(slot, step):
    other = slot ^ step
    return other, other - (other > slot).astype(jnp.int32)


def tiled_place(row, tiles):
    return (row >> 3) * (tiles * SUBLANES) + (row & (SUBLANES - 1))


def flat(ref):
    return ref.reshape(ref.shape[0] * ref.shape[1] * SUBLANES, LANES)


def upward_leaves(points, order, basis_in, held):
    rows, columns = points.shape
    leaves, leaf_rows, rank = basis_in.shape
    tiles = columns // LANES
    width = tiles + rank // LANES
    half = columns // 2
    groups = rows // SUBLANES
    chunk = 256
    count = len(held)

    def body(*refs):
        order_hbm, points_ref, basis_hbm = refs[:3]
        held_in = refs[3 : 3 + count]
        rounded_ref, hat_ref, tiled, local_ref, kept_ref, sent_ref = refs[3 + count : 9 + count]
        held_out = refs[9 + count : 9 + 2 * count]
        gathered, total, lifted, basis_ref, source_ref, order_ref = refs[
            9 + 2 * count : 15 + 2 * count
        ]
        sems, basis_sem, order_sems, held_sems = refs[15 + 2 * count :]
        order_copy = pltpu.make_async_copy(order_hbm, local_ref, order_sems.at[0])
        order_copy.start()
        copies = [
            pltpu.make_async_copy(
                points_ref.at[:, :, pl.ds(t * LANES, LANES)], tiled.at[:, t], sems.at[t]
            )
            for t in range(tiles)
        ]
        for copy in copies:
            copy.start()
        basis_copy = pltpu.make_async_copy(basis_hbm, basis_ref, basis_sem)
        basis_copy.start()
        held_copies = [
            pltpu.make_async_copy(src, dst, held_sems.at[i])
            for i, (src, dst) in enumerate(zip(held_in, held_out))
        ]
        order_copy.wait()
        row = local_row(local_ref[...], rows)
        source_ref[...] = tiled_place(row, tiles)
        local_ref[...] = tiled_place(row, width)
        source_copy = pltpu.make_async_copy(source_ref, order_ref, order_sems.at[1])
        source_copy.start()
        for copy in copies:
            copy.wait()
        for copy in held_copies:
            copy.start()
        source_copy.wait()
        basis_copy.wait()
        tiled_flat = flat(tiled)
        gathered_flat = flat(gathered)

        def take(block):
            for i in range(block * chunk, (block + 1) * chunk):
                gathered_flat[pl.ds(tiled_place(i, tiles), tiles, stride=SUBLANES), :] = tiled_flat[
                    pl.ds(order_ref[i], tiles, stride=SUBLANES), :
                ]

        def use(block):
            outer = block * chunk
            leaf = outer // leaf_rows
            inner = outer - leaf * leaf_rows
            for t in range(tiles):
                piece = gathered[outer // SUBLANES : (outer + chunk) // SUBLANES, t]
                rounded_ref[outer : outer + chunk, t * LANES : (t + 1) * LANES] = piece.reshape(
                    chunk, LANES
                ).astype(jnp.bfloat16)
            term = dot_t(
                basis_ref[leaf, inner : inner + chunk, :], rounded_ref[outer : outer + chunk, :]
            )
            if inner > 0:
                term = term + total[...]
            if inner + chunk < leaf_rows:
                total[...] = term
                return
            hat_ref[leaf] = term.astype(jnp.bfloat16)
            if leaf == 0:
                held_copies[0].wait()
            low = lax.axis_index("gz") & 1
            first = pl.multiple_of((low * leaves + leaf) * rank, rank)
            lift = dot_t(held_out[0][0, 0, pl.ds(first, rank), :], hat_ref[leaf])
            lifted[...] = lift if leaf == 0 else lifted[...] + lift

        blocks = rows // chunk
        for block in range(blocks):
            if block:
                use(block - 1)
            take(block)
        use(blocks - 1)
        low = lax.axis_index("gz") & 1
        for place, target in ((low, kept_ref), (1 - low, sent_ref)):
            cols = pl.ds(pl.multiple_of(place * half, half), half)
            target[...] = lifted[:, cols].astype(target.dtype)
        for copy in held_copies[1:]:
            copy.wait()

    hbm_spec = pl.BlockSpec(memory_space=pltpu.HBM)
    grouped = points.reshape(groups, SUBLANES, columns)
    return pl.pallas_call(
        body,
        name="upward_leaves",
        out_shape=[
            pltpu.VMEM((rows, columns), jnp.bfloat16),
            pltpu.VMEM((leaves, rank, columns), jnp.bfloat16),
            pltpu.VMEM((groups, tiles, SUBLANES, LANES), jnp.float32),
            pltpu.VMEM(order.shape, order.dtype),
            pltpu.VMEM((rank, half), jnp.float32),
            pltpu.VMEM((rank, half), jnp.bfloat16),
        ]
        + [pltpu.VMEM(h.shape, h.dtype) for h in held],
        in_specs=[hbm_spec] * (3 + count),
        out_specs=[vmem_spec()] * (6 + count),
        scratch_shapes=[
            pltpu.VMEM((groups, tiles, SUBLANES, LANES), jnp.float32),
            pltpu.VMEM((rank, columns), jnp.float32),
            pltpu.VMEM((rank, columns), jnp.float32),
            pltpu.VMEM(basis_in.shape, basis_in.dtype),
            pltpu.VMEM(order.shape, order.dtype),
            pltpu.SMEM(order.shape, order.dtype),
            pltpu.SemaphoreType.DMA((tiles,)),
            pltpu.SemaphoreType.DMA,
            pltpu.SemaphoreType.DMA((2,)),
            pltpu.SemaphoreType.DMA((count,)),
        ],
        compiler_params=pltpu.CompilerParams(vmem_limit_bytes=12 * MIB),
    )(*[stay(value) for value in (order, grouped, basis_in, *held)])


def call_small(body, out_shape, operands, scratch=(), limit=4):
    many = isinstance(out_shape, list)
    return pl.pallas_call(
        body,
        out_shape=out_shape,
        in_specs=[vmem_spec()] * len(operands),
        out_specs=[vmem_spec()] * len(out_shape) if many else vmem_spec(),
        scratch_shapes=list(scratch),
        compiler_params=pltpu.CompilerParams(vmem_limit_bytes=limit * MIB),
    )(*operands)


def first_sum(kept, arrived):
    def body(kept_ref, arrived_ref, out_ref):
        out_ref[...] = (kept_ref[...] + arrived_ref[...].astype(jnp.float32)).astype(jnp.bfloat16)

    return call_small(body, pltpu.VMEM(arrived.shape, jnp.bfloat16), [kept, arrived])


def next_lift(own, others, lifters, stage, axis, shift, after):
    rank, half = own.shape

    def body(own_ref, a_ref, b_ref, c_ref, lifter_ref, after_ref, out_ref):
        slot = slot_of(axis, shift)
        total = None
        for step, source in enumerate((own_ref, a_ref, b_ref, c_ref)):
            first = pl.multiple_of((slot ^ step) * rank, rank)
            term = dot_t(lifter_ref[0, stage + 1, pl.ds(first, rank), :], source[...])
            total = term if total is None else total + term
        out_ref[...] = total.astype(jnp.bfloat16)

    return call_small(body, pltpu.VMEM((rank, half), jnp.bfloat16), [own, *others, lifters, after])


def far_sum(sources, coupling_ref, stage, slot):
    total = None
    for step, source in enumerate(sources, 1):
        _, place = sibling(slot, step)
        term = dot(coupling_ref[0, stage, place], source[...])
        total = term if total is None else total + term
    return total


def far_of(others, couplings, stage, axis, shift, after):
    rank, half = others[0].shape

    def body(a_ref, b_ref, c_ref, coupling_ref, after_ref, out_ref):
        out_ref[...] = far_sum(
            (a_ref, b_ref, c_ref), coupling_ref, stage, slot_of(axis, shift)
        )

    return call_small(body, pltpu.VMEM((rank, half), jnp.float32), [*others, couplings, after])


def go_down(others, fars, couplings, lowers, places, after):
    rank, half = others[0].shape
    top = len(places) - 1

    def body(*refs):
        a_ref, b_ref, c_ref, coupling_ref, lower_ref = refs[:5]
        far_refs = refs[5:-2]
        value = far_sum((a_ref, b_ref, c_ref), coupling_ref, top, slot_of(*places[top]))
        for stage in range(top - 1, -1, -1):
            first = pl.multiple_of(slot_of(*places[stage]) * rank, rank)
            block = lower_ref[0, stage + 1, pl.ds(first, rank), :]
            value = far_refs[stage][...] + dot(block, value.astype(jnp.bfloat16))
        refs[-1][...] = value.astype(jnp.bfloat16)

    return call_small(
        body, pltpu.VMEM((rank, half), jnp.bfloat16), [*others, couplings, lowers, *fars, after]
    )


def local_part(rounded, own, partner, near, basis_out, leaf_coupling, lowers, local, after):
    rows, columns = rounded.shape
    leaves, leaf_rows, _ = near.shape
    rank = basis_out.shape[2]
    tiles = columns // LANES
    width = tiles + rank // LANES
    groups = rows // SUBLANES
    chunk = 256
    blocks = rows // chunk

    def body(
        near_hbm,
        rounded_ref,
        own_ref,
        partner_ref,
        basis_ref,
        coupling_ref,
        lower_ref,
        local_ref,
        after_ref,
        initial,
        tree,
        near_ref,
        children,
        order_ref,
        sems,
        order_sem,
    ):
        low = lax.axis_index("gz") & 1
        order_copy = pltpu.make_async_copy(local_ref, order_ref, order_sem)
        order_copy.start()
        copies = [
            pltpu.make_async_copy(near_hbm.at[leaf], near_ref.at[leaf], sems.at[leaf])
            for leaf in range(leaves)
        ]
        for copy in copies:
            copy.start()
        children[pl.ds(low * leaves, leaves)] = own_ref[...]
        children[pl.ds((1 - low) * leaves, leaves)] = partner_ref[...]
        tree_flat = flat(tree)
        initial_flat = flat(initial)
        fars = []

        def keep(first, size, column, value):
            for t in range(value.shape[1] // LANES):
                tree[first // SUBLANES : (first + size) // SUBLANES, column + t] = value[
                    :, t * LANES : (t + 1) * LANES
                ].reshape(size // SUBLANES, SUBLANES, LANES)

        for leaf in range(leaves):
            slot = low * leaves + leaf
            far = None
            for t in range(ARITY - 1):
                source = t + (t >= slot).astype(jnp.int32)
                term = dot(coupling_ref[leaf, t], children[source])
                far = term if far is None else far + term
            fars.append(far.astype(jnp.bfloat16))
            lower = lower_ref[0, 0, pl.ds(pl.multiple_of(slot * rank, rank), rank), :]
            keep(leaf * leaf_rows, leaf_rows, tiles, dot(basis_ref[leaf], lower))
        order_copy.wait()

        def compute(block):
            outer = block * chunk
            leaf = outer // leaf_rows
            inner = outer - leaf * leaf_rows
            if inner == 0:
                copies[leaf].wait()
            values = rounded_ref[leaf * leaf_rows : (leaf + 1) * leaf_rows, :]
            value = dot(near_ref[leaf, inner : inner + chunk, :], values)
            value = value + dot(basis_ref[leaf, inner : inner + chunk, :], fars[leaf])
            keep(outer, chunk, 0, value)

        def scatter(block):
            for i in range(block * chunk, (block + 1) * chunk):
                initial_flat[pl.ds(order_ref[i], width, stride=SUBLANES), :] = tree_flat[
                    pl.ds(tiled_place(i, width), width, stride=SUBLANES), :
                ]

        for block in range(blocks):
            compute(block)
            if block:
                scatter(block - 1)
        scatter(blocks - 1)

    hbm_spec = pl.BlockSpec(memory_space=pltpu.HBM)
    return pl.pallas_call(
        body,
        name="local_part",
        out_shape=pltpu.VMEM((groups, width, SUBLANES, LANES), jnp.float32),
        in_specs=[hbm_spec] + [vmem_spec()] * 8,
        out_specs=vmem_spec(),
        scratch_shapes=[
            pltpu.VMEM((groups, width, SUBLANES, LANES), jnp.float32),
            pltpu.VMEM(near.shape, near.dtype),
            pltpu.VMEM((ARITY, rank, columns), jnp.bfloat16),
            pltpu.SMEM(local.shape, local.dtype),
            pltpu.SemaphoreType.DMA((leaves,)),
            pltpu.SemaphoreType.DMA,
        ],
        compiler_params=pltpu.CompilerParams(vmem_limit_bytes=16 * MIB),
    )(stay(near), rounded, own, partner, basis_out, leaf_coupling, lowers, local, after)


def to_rows(initial, tiled, ridge, after):
    groups, width, _, _ = initial.shape
    tiles = tiled.shape[1]
    rows = groups * SUBLANES
    rank = (width - tiles) * LANES
    chunk = 256
    size = chunk // SUBLANES

    def body(ridge_ref, initial_ref, tiled_ref, after_ref, base_ref, spread_ref):
        ridge_value = ridge_ref[0]

        def spread(block, _):
            group = pl.ds(block * size, size)
            for t in range(tiles):
                base_ref[group, t] = initial_ref[group, t] + ridge_value * tiled_ref[group, t]
            first = pl.multiple_of(block * chunk, chunk)
            for t in range(width - tiles):
                spread_ref[pl.ds(first, chunk), t * LANES : (t + 1) * LANES] = (
                    initial_ref[group, tiles + t].reshape(chunk, LANES).astype(jnp.bfloat16)
                )
            return 0

        lax.fori_loop(0, rows // chunk, spread, 0)

    smem_spec = pl.BlockSpec(memory_space=pltpu.SMEM)
    return pl.pallas_call(
        body,
        name="to_rows",
        out_shape=[
            pltpu.VMEM(tiled.shape, jnp.float32),
            pltpu.VMEM((rows, rank), jnp.bfloat16),
        ],
        in_specs=[smem_spec] + [vmem_spec()] * 3,
        out_specs=[vmem_spec()] * 2,
        compiler_params=pltpu.CompilerParams(vmem_limit_bytes=4 * MIB),
    )(ridge, initial, tiled, after)


def finish(base, spread, lowered, other, previous):
    groups, tiles, _, _ = base.shape
    rows = groups * SUBLANES
    half = tiles // 2
    parts = 4
    step = rows // parts
    size = step // SUBLANES

    def body(*refs):
        base_ref, spread_ref, lowered_ref = refs[:3]
        out_ref, result, sems = refs[-3:]
        place = lax.axis_index("gz") & 1
        if other:
            place = 1 - place
        copies = []
        for p in range(parts):
            group = slice(p * size, (p + 1) * size)
            value = dot(spread_ref[p * step : (p + 1) * step, :], lowered_ref[...])
            for t in range(half):
                result[t, group] = base_ref[group, place * half + t] + value[
                    :, t * LANES : (t + 1) * LANES
                ].reshape(size, SUBLANES, LANES)
            for t in range(half):
                column = pl.multiple_of((place * half + t) * LANES, LANES)
                copy = pltpu.make_async_copy(
                    result.at[t, pl.ds(p * size, size)],
                    out_ref.at[pl.ds(p * size, size), :, pl.ds(column, LANES)],
                    sems.at[p * half + t],
                )
                copy.start()
                copies.append(copy)
        for copy in copies:
            copy.wait()

    hbm_spec = pl.BlockSpec(memory_space=pltpu.HBM)
    extra = [] if previous is None else [previous]
    return pl.pallas_call(
        body,
        name="finish_other" if other else "finish_own",
        out_shape=pltpu.HBM((groups, SUBLANES, tiles * LANES), jnp.float32),
        in_specs=[vmem_spec()] * 3 + [hbm_spec] * len(extra),
        out_specs=hbm_spec,
        scratch_shapes=[
            pltpu.VMEM((half, groups, SUBLANES, LANES), jnp.float32),
            pltpu.SemaphoreType.DMA((parts * half,)),
        ],
        input_output_aliases={3: 0} if extra else {},
        compiler_params=pltpu.CompilerParams(vmem_limit_bytes=4 * MIB),
    )(base, spread, lowered, *extra)


def swap(value, axis, mask):
    size = lax.axis_size(axis)
    return lax.ppermute(value, axis, [(s, s ^ mask) for s in range(size)])


def on_device(
    points,
    order,
    near,
    basis_in,
    basis_out,
    leaf_coupling,
    transfer_up,
    transfer_down,
    node_coupling,
    ridge,
):
    stages = transfer_up.shape[1]
    places = [("gz", 1 + 2 * i) for i in range(stages - 2)] + [("gy", 0), ("gx", 0)]
    held = [transfer_up, leaf_coupling, basis_out, transfer_down, node_coupling]
    rounded, leaf_hat, tiled, local, part, sent, *kept = upward_leaves(
        points, order, basis_in, held
    )
    lifters, leaf_couplings, bases, lowers, couplings = kept
    hat = first_sum(part, swap(sent, "gz", 1))
    fars = []
    for stage, (axis, shift) in enumerate(places):
        others = [None] * (ARITY - 1)
        for step in STEPS:
            others[step - 1] = swap(hat, axis, step << shift)
        if stage == 0:
            leaf_hat, _ = lax.optimization_barrier((leaf_hat, hat))
            partner_hat = swap(leaf_hat, "gz", 1)
            initial = local_part(
                rounded, leaf_hat, partner_hat, near, bases, leaf_couplings, lowers, local, hat
            )
            after = initial
        if stage == 1:
            base, spread = to_rows(initial, tiled, ridge, hat)
        if stage + 1 < stages:
            hat = next_lift(hat, others, lifters, stage, axis, shift, after)
            after = hat
            fars.append(far_of(others, couplings, stage, axis, shift, hat))
    value = go_down(others, fars, couplings, lowers, places, spread)
    partner_value = swap(value, "gz", 1)
    result = finish(base, spread, value, False, None)
    result = finish(base, spread, partner_value, True, result)
    return result.reshape(points.shape)


def solution(mesh):
    placed = (
        P(("gx", "gy", "gz"), None),
        P(("gx", "gy", "gz")),
        P(("gx", "gy", "gz"), None, None),
        P(("gx", "gy", "gz"), None, None),
        P(("gx", "gy", "gz"), None, None),
        P(("gx", "gy", "gz"), None, None, None),
        P(("gx", "gy", "gz"), None, None, None),
        P(("gx", "gy", "gz"), None, None, None),
        P(("gx", "gy", "gz"), None, None, None, None),
        P(),
    )

    return jax.shard_map(
        on_device,
        mesh=mesh,
        in_specs=placed,
        out_specs=P(("gx", "gy", "gz"), None),
        check_vma=False,
    )
```

```python
import jax
import jax.numpy as jnp
from jax import lax
from jax.experimental import pallas as pl
from jax.experimental.pallas import tpu as pltpu
from jax.sharding import PartitionSpec as P


LANES = 128
ARITY = 4
STEPS = {"gz": (2, 1, 3), "gy": (2, 1, 3), "gx": (1, 2, 3)}
SUBLANES = 8
MIB = 1 << 20


def vmem_spec():
    return pl.BlockSpec(memory_space=pltpu.VMEM)


def stay(value):
    return pltpu.with_memory_space_constraint(value, pltpu.HBM)


def dot(left, right):
    return jnp.dot(left, right, preferred_element_type=jnp.float32)


def dot_t(left, right):
    return lax.dot_general(
        left, right, (((0,), (0,)), ((), ())), preferred_element_type=jnp.float32
    )


def local_row(value, rows):
    if rows & (rows - 1) == 0:
        return value & (rows - 1)
    return lax.rem(value, rows)


def slot_of(axis, shift):
    return (lax.axis_index(axis) >> shift) & (ARITY - 1)


def sibling(slot, step):
    other = slot ^ step
    return other, other - (other > slot).astype(jnp.int32)


def tiled_place(row, tiles):
    return (row >> 3) * (tiles * SUBLANES) + (row & (SUBLANES - 1))


def flat(ref):
    return ref.reshape(ref.shape[0] * ref.shape[1] * SUBLANES, LANES)


def wide(ref, first, size):
    return jnp.concatenate([ref[t, first : first + size, :] for t in range(ref.shape[0])], axis=1)


def upward_leaves(points, order, basis_in, held):
    rows, columns = points.shape
    leaves, leaf_rows, rank = basis_in.shape
    tiles = columns // LANES
    width = tiles + rank // LANES
    half = columns // 2
    groups = rows // SUBLANES
    large = 512
    count = len(held)

    def body(*refs):
        order_hbm, points_ref, basis_hbm = refs[:3]
        held_in = refs[3 : 3 + count]
        rounded_ref, hat_ref, tiled, local_ref, kept_ref, sent_ref = refs[3 + count : 9 + count]
        held_out = refs[9 + count : 9 + 2 * count]
        gathered, total, lifted, basis_ref, source_ref, order_ref = refs[
            9 + 2 * count : 15 + 2 * count
        ]
        sems, basis_sem, order_sems, held_sems = refs[15 + 2 * count :]
        order_copy = pltpu.make_async_copy(order_hbm, local_ref, order_sems.at[0])
        order_copy.start()
        copies = [
            pltpu.make_async_copy(
                points_ref.at[:, :, pl.ds(t * LANES, LANES)], tiled.at[:, t], sems.at[t]
            )
            for t in range(tiles)
        ]
        for copy in copies:
            copy.start()
        basis_copy = pltpu.make_async_copy(basis_hbm, basis_ref, basis_sem)
        basis_copy.start()
        held_copies = [
            pltpu.make_async_copy(src, dst, held_sems.at[i])
            for i, (src, dst) in enumerate(zip(held_in, held_out))
        ]
        order_copy.wait()
        row = local_row(local_ref[...], rows)
        source_ref[...] = tiled_place(row, tiles)
        local_ref[...] = tiled_place(row, width)
        source_copy = pltpu.make_async_copy(source_ref, order_ref, order_sems.at[1])
        source_copy.start()
        for copy in copies:
            copy.wait()
        for copy in held_copies:
            copy.start()
        source_copy.wait()
        basis_copy.wait()
        tiled_flat = flat(tiled)
        gathered_flat = flat(gathered)

        def take(outer, chunk):
            for i in range(outer, outer + chunk):
                gathered_flat[pl.ds(tiled_place(i, tiles), tiles, stride=SUBLANES), :] = tiled_flat[
                    pl.ds(order_ref[i], tiles, stride=SUBLANES), :
                ]

        def use(outer, chunk):
            leaf = outer // leaf_rows
            inner = outer - leaf * leaf_rows
            for t in range(tiles):
                piece = gathered[outer // SUBLANES : (outer + chunk) // SUBLANES, t]
                rounded_ref[t, outer : outer + chunk, :] = piece.reshape(chunk, LANES).astype(
                    jnp.bfloat16
                )
            term = dot_t(
                basis_ref[leaf, inner : inner + chunk, :], wide(rounded_ref, outer, chunk)
            )
            if inner > 0:
                term = term + total[...]
            if inner + chunk < leaf_rows:
                total[...] = term
                return
            hat_ref[leaf] = term.astype(jnp.bfloat16)
            if leaf == 0:
                held_copies[0].wait()
            low = lax.axis_index("gz") & 1
            first = pl.multiple_of((low * leaves + leaf) * rank, rank)
            lift = dot_t(held_out[0][0, 0, pl.ds(first, rank), :], hat_ref[leaf])
            lifted[...] = lift if leaf == 0 else lifted[...] + lift

        pieces = [(first, large) for first in range(0, rows, large)]
        pieces[-1:] = [(rows - large, large // 2), (rows - large // 2, large // 2)]
        for k, piece in enumerate(pieces):
            if k:
                use(*pieces[k - 1])
            take(*piece)
        use(*pieces[-1])
        low = lax.axis_index("gz") & 1
        for place, target in ((low, kept_ref), (1 - low, sent_ref)):
            cols = pl.ds(pl.multiple_of(place * half, half), half)
            target[...] = lifted[:, cols].astype(target.dtype)
        for copy in held_copies[1:]:
            copy.wait()

    hbm_spec = pl.BlockSpec(memory_space=pltpu.HBM)
    grouped = points.reshape(groups, SUBLANES, columns)
    return pl.pallas_call(
        body,
        name="upward_leaves",
        out_shape=[
            pltpu.VMEM((tiles, rows, LANES), jnp.bfloat16),
            pltpu.VMEM((leaves, rank, columns), jnp.bfloat16),
            pltpu.VMEM((groups, tiles, SUBLANES, LANES), jnp.float32),
            pltpu.VMEM(order.shape, order.dtype),
            pltpu.VMEM((rank, half), jnp.float32),
            pltpu.VMEM((rank, half), jnp.bfloat16),
        ]
        + [pltpu.VMEM(h.shape, h.dtype) for h in held],
        in_specs=[hbm_spec] * (3 + count),
        out_specs=[vmem_spec()] * (6 + count),
        scratch_shapes=[
            pltpu.VMEM((groups, tiles, SUBLANES, LANES), jnp.float32),
            pltpu.VMEM((rank, columns), jnp.float32),
            pltpu.VMEM((rank, columns), jnp.float32),
            pltpu.VMEM(basis_in.shape, basis_in.dtype),
            pltpu.VMEM(order.shape, order.dtype),
            pltpu.SMEM(order.shape, order.dtype),
            pltpu.SemaphoreType.DMA((tiles,)),
            pltpu.SemaphoreType.DMA,
            pltpu.SemaphoreType.DMA((2,)),
            pltpu.SemaphoreType.DMA((count,)),
        ],
        compiler_params=pltpu.CompilerParams(vmem_limit_bytes=12 * MIB),
    )(*[stay(value) for value in (order, grouped, basis_in, *held)])


def call_small(body, out_shape, operands, scratch=(), limit=4):
    many = isinstance(out_shape, list)
    return pl.pallas_call(
        body,
        out_shape=out_shape,
        in_specs=[vmem_spec()] * len(operands),
        out_specs=[vmem_spec()] * len(out_shape) if many else vmem_spec(),
        scratch_shapes=list(scratch),
        compiler_params=pltpu.CompilerParams(vmem_limit_bytes=limit * MIB),
    )(*operands)


def first_sum(kept, arrived):
    def body(kept_ref, arrived_ref, out_ref):
        out_ref[...] = (kept_ref[...] + arrived_ref[...].astype(jnp.float32)).astype(jnp.bfloat16)

    return call_small(body, pltpu.VMEM(arrived.shape, jnp.bfloat16), [kept, arrived])


def next_lift(own, others, lifters, stage, axis, shift, after):
    rank, half = own.shape

    def body(own_ref, a_ref, b_ref, c_ref, lifter_ref, after_ref, out_ref):
        slot = slot_of(axis, shift)
        total = None
        for step, source in enumerate((own_ref, a_ref, b_ref, c_ref)):
            first = pl.multiple_of((slot ^ step) * rank, rank)
            term = dot_t(lifter_ref[0, stage + 1, pl.ds(first, rank), :], source[...])
            total = term if total is None else total + term
        out_ref[...] = total.astype(jnp.bfloat16)

    return call_small(body, pltpu.VMEM((rank, half), jnp.bfloat16), [own, *others, lifters, after])


def far_sum(sources, coupling_ref, stage, slot):
    total = None
    for step, source in enumerate(sources, 1):
        _, place = sibling(slot, step)
        term = dot(coupling_ref[0, stage, place], source[...])
        total = term if total is None else total + term
    return total


def far_of(others, couplings, stage, axis, shift, after):
    rank, half = others[0].shape

    def body(a_ref, b_ref, c_ref, coupling_ref, after_ref, out_ref):
        out_ref[...] = far_sum(
            (a_ref, b_ref, c_ref), coupling_ref, stage, slot_of(axis, shift)
        )

    return call_small(body, pltpu.VMEM((rank, half), jnp.float32), [*others, couplings, after])


def go_down(others, fars, couplings, lowers, places, after):
    rank, half = others[0].shape
    top = len(places) - 1

    def body(*refs):
        a_ref, b_ref, c_ref, coupling_ref, lower_ref = refs[:5]
        far_refs = refs[5:-2]
        value = far_sum((a_ref, b_ref, c_ref), coupling_ref, top, slot_of(*places[top]))
        for stage in range(top - 1, -1, -1):
            first = pl.multiple_of(slot_of(*places[stage]) * rank, rank)
            block = lower_ref[0, stage + 1, pl.ds(first, rank), :]
            value = far_refs[stage][...] + dot(block, value.astype(jnp.bfloat16))
        refs[-1][...] = value.astype(jnp.bfloat16)

    return call_small(
        body, pltpu.VMEM((rank, half), jnp.bfloat16), [*others, couplings, lowers, *fars, after]
    )


def local_part(rounded, own, partner, near, basis_out, leaf_coupling, lowers, local, after):
    tiles, rows, _ = rounded.shape
    columns = tiles * LANES
    leaves, leaf_rows, _ = near.shape
    rank = basis_out.shape[2]
    width = tiles + rank // LANES
    groups = rows // SUBLANES
    chunk = 256
    blocks = rows // chunk

    def body(
        near_hbm,
        rounded_ref,
        own_ref,
        partner_ref,
        basis_ref,
        coupling_ref,
        lower_ref,
        local_ref,
        after_ref,
        initial,
        tree,
        near_ref,
        children,
        order_ref,
        sems,
        order_sem,
    ):
        low = lax.axis_index("gz") & 1
        order_copy = pltpu.make_async_copy(local_ref, order_ref, order_sem)
        order_copy.start()
        copies = [
            pltpu.make_async_copy(near_hbm.at[leaf], near_ref.at[leaf], sems.at[leaf])
            for leaf in range(leaves)
        ]
        for copy in copies:
            copy.start()
        children[pl.ds(low * leaves, leaves)] = own_ref[...]
        children[pl.ds((1 - low) * leaves, leaves)] = partner_ref[...]
        tree_flat = flat(tree)
        initial_flat = flat(initial)
        fars = []

        def keep(first, size, column, value):
            for t in range(value.shape[1] // LANES):
                tree[first // SUBLANES : (first + size) // SUBLANES, column + t] = value[
                    :, t * LANES : (t + 1) * LANES
                ].reshape(size // SUBLANES, SUBLANES, LANES)

        for leaf in range(leaves):
            slot = low * leaves + leaf
            far = None
            for t in range(ARITY - 1):
                source = t + (t >= slot).astype(jnp.int32)
                term = dot(coupling_ref[leaf, t], children[source])
                far = term if far is None else far + term
            fars.append(far.astype(jnp.bfloat16))
            lower = lower_ref[0, 0, pl.ds(pl.multiple_of(slot * rank, rank), rank), :]
            keep(leaf * leaf_rows, leaf_rows, tiles, dot(basis_ref[leaf], lower))
        order_copy.wait()

        def compute(block):
            outer = block * chunk
            leaf = outer // leaf_rows
            inner = outer - leaf * leaf_rows
            if inner == 0:
                copies[leaf].wait()
            values = wide(rounded_ref, leaf * leaf_rows, leaf_rows)
            value = dot(near_ref[leaf, inner : inner + chunk, :], values)
            value = value + dot(basis_ref[leaf, inner : inner + chunk, :], fars[leaf])
            keep(outer, chunk, 0, value)

        def scatter(block):
            for i in range(block * chunk, (block + 1) * chunk):
                initial_flat[pl.ds(order_ref[i], width, stride=SUBLANES), :] = tree_flat[
                    pl.ds(tiled_place(i, width), width, stride=SUBLANES), :
                ]

        for block in range(blocks):
            compute(block)
            if block:
                scatter(block - 1)
        scatter(blocks - 1)

    hbm_spec = pl.BlockSpec(memory_space=pltpu.HBM)
    return pl.pallas_call(
        body,
        name="local_part",
        out_shape=pltpu.VMEM((groups, width, SUBLANES, LANES), jnp.float32),
        in_specs=[hbm_spec] + [vmem_spec()] * 8,
        out_specs=vmem_spec(),
        scratch_shapes=[
            pltpu.VMEM((groups, width, SUBLANES, LANES), jnp.float32),
            pltpu.VMEM(near.shape, near.dtype),
            pltpu.VMEM((ARITY, rank, columns), jnp.bfloat16),
            pltpu.SMEM(local.shape, local.dtype),
            pltpu.SemaphoreType.DMA((leaves,)),
            pltpu.SemaphoreType.DMA,
        ],
        compiler_params=pltpu.CompilerParams(vmem_limit_bytes=16 * MIB),
    )(stay(near), rounded, own, partner, basis_out, leaf_coupling, lowers, local, after)


def to_rows(initial, tiled, ridge, after):
    groups, width, _, _ = initial.shape
    tiles = tiled.shape[1]
    rows = groups * SUBLANES
    rank = (width - tiles) * LANES
    chunk = 256
    size = chunk // SUBLANES

    def body(ridge_ref, initial_ref, tiled_ref, after_ref, base_ref, spread_ref):
        ridge_value = ridge_ref[0]

        def spread(block, _):
            group = pl.ds(block * size, size)
            for t in range(tiles):
                base_ref[group, t] = initial_ref[group, t] + ridge_value * tiled_ref[group, t]
            first = pl.multiple_of(block * chunk, chunk)
            for t in range(width - tiles):
                spread_ref[pl.ds(first, chunk), t * LANES : (t + 1) * LANES] = (
                    initial_ref[group, tiles + t].reshape(chunk, LANES).astype(jnp.bfloat16)
                )
            return 0

        lax.fori_loop(0, rows // chunk, spread, 0)

    smem_spec = pl.BlockSpec(memory_space=pltpu.SMEM)
    return pl.pallas_call(
        body,
        name="to_rows",
        out_shape=[
            pltpu.VMEM(tiled.shape, jnp.float32),
            pltpu.VMEM((rows, rank), jnp.bfloat16),
        ],
        in_specs=[smem_spec] + [vmem_spec()] * 3,
        out_specs=[vmem_spec()] * 2,
        compiler_params=pltpu.CompilerParams(vmem_limit_bytes=4 * MIB),
    )(ridge, initial, tiled, after)


def finish(base, spread, lowered, other, previous):
    groups, tiles, _, _ = base.shape
    rows = groups * SUBLANES
    half = tiles // 2
    parts = 4
    step = rows // parts
    size = step // SUBLANES

    def body(*refs):
        base_ref, spread_ref, lowered_ref = refs[:3]
        out_ref, result, sems = refs[-3:]
        place = lax.axis_index("gz") & 1
        if other:
            place = 1 - place
        copies = []
        for p in range(parts):
            group = slice(p * size, (p + 1) * size)
            value = dot(spread_ref[p * step : (p + 1) * step, :], lowered_ref[...])
            for t in range(half):
                result[t, group] = base_ref[group, place * half + t] + value[
                    :, t * LANES : (t + 1) * LANES
                ].reshape(size, SUBLANES, LANES)
            for t in range(half):
                column = pl.multiple_of((place * half + t) * LANES, LANES)
                copy = pltpu.make_async_copy(
                    result.at[t, pl.ds(p * size, size)],
                    out_ref.at[pl.ds(p * size, size), :, pl.ds(column, LANES)],
                    sems.at[p * half + t],
                )
                copy.start()
                copies.append(copy)
        for copy in copies:
            copy.wait()

    hbm_spec = pl.BlockSpec(memory_space=pltpu.HBM)
    extra = [] if previous is None else [previous]
    return pl.pallas_call(
        body,
        name="finish_other" if other else "finish_own",
        out_shape=pltpu.HBM((groups, SUBLANES, tiles * LANES), jnp.float32),
        in_specs=[vmem_spec()] * 3 + [hbm_spec] * len(extra),
        out_specs=hbm_spec,
        scratch_shapes=[
            pltpu.VMEM((half, groups, SUBLANES, LANES), jnp.float32),
            pltpu.SemaphoreType.DMA((parts * half,)),
        ],
        input_output_aliases={3: 0} if extra else {},
        compiler_params=pltpu.CompilerParams(vmem_limit_bytes=4 * MIB),
    )(base, spread, lowered, *extra)


def swap(value, axis, mask):
    size = lax.axis_size(axis)
    return lax.ppermute(value, axis, [(s, s ^ mask) for s in range(size)])


def on_device(
    points,
    order,
    near,
    basis_in,
    basis_out,
    leaf_coupling,
    transfer_up,
    transfer_down,
    node_coupling,
    ridge,
):
    stages = transfer_up.shape[1]
    places = [("gz", 1 + 2 * i) for i in range(stages - 2)] + [("gy", 0), ("gx", 0)]
    held = [transfer_up, leaf_coupling, basis_out, transfer_down, node_coupling]
    rounded, leaf_hat, tiled, local, part, sent, *kept = upward_leaves(
        points, order, basis_in, held
    )
    lifters, leaf_couplings, bases, lowers, couplings = kept
    hat = first_sum(part, swap(sent, "gz", 1))
    fars = []
    for stage, (axis, shift) in enumerate(places):
        others = [None] * (ARITY - 1)
        for step in STEPS[axis]:
            others[step - 1] = swap(hat, axis, step << shift)
        if stage == 0:
            leaf_hat, _ = lax.optimization_barrier((leaf_hat, hat))
            partner_hat = swap(leaf_hat, "gz", 1)
            initial = local_part(
                rounded, leaf_hat, partner_hat, near, bases, leaf_couplings, lowers, local, hat
            )
            after = initial
        if stage == 1:
            base, spread = to_rows(initial, tiled, ridge, hat)
        if stage + 1 < stages:
            hat = next_lift(hat, others, lifters, stage, axis, shift, after)
            after = hat
            fars.append(far_of(others, couplings, stage, axis, shift, hat))
    value = go_down(others, fars, couplings, lowers, places, spread)
    partner_value = swap(value, "gz", 1)
    result = finish(base, spread, value, False, None)
    result = finish(base, spread, partner_value, True, result)
    return result.reshape(points.shape)


def solution(mesh):
    placed = (
        P(("gx", "gy", "gz"), None),
        P(("gx", "gy", "gz")),
        P(("gx", "gy", "gz"), None, None),
        P(("gx", "gy", "gz"), None, None),
        P(("gx", "gy", "gz"), None, None),
        P(("gx", "gy", "gz"), None, None, None),
        P(("gx", "gy", "gz"), None, None, None),
        P(("gx", "gy", "gz"), None, None, None),
        P(("gx", "gy", "gz"), None, None, None, None),
        P(),
    )

    return jax.shard_map(
        on_device,
        mesh=mesh,
        in_specs=placed,
        out_specs=P(("gx", "gy", "gz"), None),
        check_vma=False,
    )
```

```python
import jax
import jax.numpy as jnp
from jax import lax
from jax.experimental import pallas as pl
from jax.experimental.pallas import tpu as pltpu
from jax.sharding import PartitionSpec as P


LANES = 128
ARITY = 4
CORE_STEPS = {("gx", 1): (1, 2), ("gx", 2): (2, 1)}
STEPS = {"gz": (2, 1, 3), "gy": (2, 1, 3), "gx": (1, 2, 3)}
SUBLANES = 8
MIB = 1 << 20


def vmem_spec():
    return pl.BlockSpec(memory_space=pltpu.VMEM)


def stay(value):
    return pltpu.with_memory_space_constraint(value, pltpu.HBM)


def dot(left, right):
    return jnp.dot(left, right, preferred_element_type=jnp.float32)


def dot_t(left, right):
    return lax.dot_general(
        left, right, (((0,), (0,)), ((), ())), preferred_element_type=jnp.float32
    )


def local_row(value, rows):
    if rows & (rows - 1) == 0:
        return value & (rows - 1)
    return lax.rem(value, rows)


def slot_of(axis, shift):
    return (lax.axis_index(axis) >> shift) & (ARITY - 1)


def steps_of(axis, number):
    return CORE_STEPS.get((axis, number), (number, number))


def sibling(slot, step):
    other = slot ^ step
    return other, other - (other > slot).astype(jnp.int32)


def tiled_place(row, tiles):
    return (row >> 3) * (tiles * SUBLANES) + (row & (SUBLANES - 1))


def flat(ref):
    return ref.reshape(ref.shape[0] * ref.shape[1] * SUBLANES, LANES)


def wide(ref, first, size):
    return jnp.concatenate([ref[t, first : first + size, :] for t in range(ref.shape[0])], axis=1)


def upward_leaves(points, order, basis_in, held):
    rows, columns = points.shape
    leaves, leaf_rows, rank = basis_in.shape
    tiles = columns // LANES
    width = tiles + rank // LANES
    half = columns // 2
    groups = rows // SUBLANES
    large = 512
    count = len(held)

    def body(*refs):
        order_hbm, points_ref, basis_hbm = refs[:3]
        held_in = refs[3 : 3 + count]
        rounded_ref, hat_ref, tiled, local_ref, kept_ref, sent_ref = refs[3 + count : 9 + count]
        held_out = refs[9 + count : 9 + 2 * count]
        gathered, total, lifted, basis_ref, source_ref, order_ref = refs[
            9 + 2 * count : 15 + 2 * count
        ]
        sems, basis_sem, order_sems, held_sems = refs[15 + 2 * count :]
        order_copy = pltpu.make_async_copy(order_hbm, local_ref, order_sems.at[0])
        order_copy.start()
        copies = [
            pltpu.make_async_copy(
                points_ref.at[:, :, pl.ds(t * LANES, LANES)], tiled.at[:, t], sems.at[t]
            )
            for t in range(tiles)
        ]
        for copy in copies:
            copy.start()
        basis_copy = pltpu.make_async_copy(basis_hbm, basis_ref, basis_sem)
        basis_copy.start()
        held_copies = [
            pltpu.make_async_copy(src, dst, held_sems.at[i])
            for i, (src, dst) in enumerate(zip(held_in, held_out))
        ]
        order_copy.wait()
        row = local_row(local_ref[...], rows)
        source_ref[...] = tiled_place(row, tiles)
        local_ref[...] = tiled_place(row, width)
        source_copy = pltpu.make_async_copy(source_ref, order_ref, order_sems.at[1])
        source_copy.start()
        for copy in copies:
            copy.wait()
        for copy in held_copies:
            copy.start()
        source_copy.wait()
        basis_copy.wait()
        tiled_flat = flat(tiled)
        gathered_flat = flat(gathered)

        def take(outer, chunk):
            for i in range(outer, outer + chunk):
                gathered_flat[pl.ds(tiled_place(i, tiles), tiles, stride=SUBLANES), :] = tiled_flat[
                    pl.ds(order_ref[i], tiles, stride=SUBLANES), :
                ]

        def use(outer, chunk):
            leaf = outer // leaf_rows
            inner = outer - leaf * leaf_rows
            for t in range(tiles):
                piece = gathered[outer // SUBLANES : (outer + chunk) // SUBLANES, t]
                rounded_ref[t, outer : outer + chunk, :] = piece.reshape(chunk, LANES).astype(
                    jnp.bfloat16
                )
            term = dot_t(
                basis_ref[leaf, inner : inner + chunk, :], wide(rounded_ref, outer, chunk)
            )
            if inner > 0:
                term = term + total[...]
            if inner + chunk < leaf_rows:
                total[...] = term
                return
            hat_ref[leaf] = term.astype(jnp.bfloat16)
            if leaf == 0:
                held_copies[0].wait()
            low = lax.axis_index("gz") & 1
            first = pl.multiple_of((low * leaves + leaf) * rank, rank)
            lift = dot_t(held_out[0][0, 0, pl.ds(first, rank), :], hat_ref[leaf])
            lifted[...] = lift if leaf == 0 else lifted[...] + lift

        pieces = [(first, large) for first in range(0, rows, large)]
        pieces[-1:] = [(rows - large, large // 2), (rows - large // 2, large // 2)]
        for k, piece in enumerate(pieces):
            if k:
                use(*pieces[k - 1])
            take(*piece)
        use(*pieces[-1])
        low = lax.axis_index("gz") & 1
        for place, target in ((low, kept_ref), (1 - low, sent_ref)):
            cols = pl.ds(pl.multiple_of(place * half, half), half)
            target[...] = lifted[:, cols].astype(target.dtype)
        for copy in held_copies[1:]:
            copy.wait()

    hbm_spec = pl.BlockSpec(memory_space=pltpu.HBM)
    grouped = points.reshape(groups, SUBLANES, columns)
    return pl.pallas_call(
        body,
        name="upward_leaves",
        out_shape=[
            pltpu.VMEM((tiles, rows, LANES), jnp.bfloat16),
            pltpu.VMEM((leaves, rank, columns), jnp.bfloat16),
            pltpu.VMEM((groups, tiles, SUBLANES, LANES), jnp.float32),
            pltpu.VMEM(order.shape, order.dtype),
            pltpu.VMEM((rank, half), jnp.float32),
            pltpu.VMEM((rank, half), jnp.bfloat16),
        ]
        + [pltpu.VMEM(h.shape, h.dtype) for h in held],
        in_specs=[hbm_spec] * (3 + count),
        out_specs=[vmem_spec()] * (6 + count),
        scratch_shapes=[
            pltpu.VMEM((groups, tiles, SUBLANES, LANES), jnp.float32),
            pltpu.VMEM((rank, columns), jnp.float32),
            pltpu.VMEM((rank, columns), jnp.float32),
            pltpu.VMEM(basis_in.shape, basis_in.dtype),
            pltpu.VMEM(order.shape, order.dtype),
            pltpu.SMEM(order.shape, order.dtype),
            pltpu.SemaphoreType.DMA((tiles,)),
            pltpu.SemaphoreType.DMA,
            pltpu.SemaphoreType.DMA((2,)),
            pltpu.SemaphoreType.DMA((count,)),
        ],
        compiler_params=pltpu.CompilerParams(vmem_limit_bytes=12 * MIB),
    )(*[stay(value) for value in (order, grouped, basis_in, *held)])


def call_small(body, out_shape, operands, scratch=(), limit=4):
    many = isinstance(out_shape, list)
    return pl.pallas_call(
        body,
        out_shape=out_shape,
        in_specs=[vmem_spec()] * len(operands),
        out_specs=[vmem_spec()] * len(out_shape) if many else vmem_spec(),
        scratch_shapes=list(scratch),
        compiler_params=pltpu.CompilerParams(vmem_limit_bytes=limit * MIB),
    )(*operands)


def first_sum(kept, arrived):
    def body(kept_ref, arrived_ref, out_ref):
        out_ref[...] = (kept_ref[...] + arrived_ref[...].astype(jnp.float32)).astype(jnp.bfloat16)

    return call_small(body, pltpu.VMEM(arrived.shape, jnp.bfloat16), [kept, arrived])


def next_lift(own, others, lifters, stage, axis, shift, after):
    rank, half = own.shape

    def body(own_ref, a_ref, b_ref, c_ref, lifter_ref, after_ref, out_ref):
        slot = slot_of(axis, shift)
        total = None
        for step, source in enumerate((own_ref, a_ref, b_ref, c_ref)):
            first = pl.multiple_of((slot ^ step) * rank, rank)
            term = dot_t(lifter_ref[0, stage + 1, pl.ds(first, rank), :], source[...])
            total = term if total is None else total + term
        out_ref[...] = total.astype(jnp.bfloat16)

    return call_small(body, pltpu.VMEM((rank, half), jnp.bfloat16), [own, *others, lifters, after])


def far_sum(sources, coupling_ref, stage, axis, shift):
    slot = slot_of(axis, shift)
    low = lax.axis_index("gz") & 1
    total = None
    for number, source in enumerate(sources, 1):
        even, odd = steps_of(axis, number)
        _, place = sibling(slot, even + low * (odd - even))
        term = dot(coupling_ref[0, stage, place], source[...])
        total = term if total is None else total + term
    return total


def far_of(others, couplings, stage, axis, shift, after):
    rank, half = others[0].shape

    def body(a_ref, b_ref, c_ref, coupling_ref, after_ref, out_ref):
        out_ref[...] = far_sum((a_ref, b_ref, c_ref), coupling_ref, stage, axis, shift)

    return call_small(body, pltpu.VMEM((rank, half), jnp.float32), [*others, couplings, after])


def go_down(others, fars, couplings, lowers, places, after):
    rank, half = others[0].shape
    top = len(places) - 1

    def body(*refs):
        a_ref, b_ref, c_ref, coupling_ref, lower_ref = refs[:5]
        far_refs = refs[5:-2]
        value = far_sum((a_ref, b_ref, c_ref), coupling_ref, top, *places[top])
        for stage in range(top - 1, -1, -1):
            first = pl.multiple_of(slot_of(*places[stage]) * rank, rank)
            block = lower_ref[0, stage + 1, pl.ds(first, rank), :]
            value = far_refs[stage][...] + dot(block, value.astype(jnp.bfloat16))
        refs[-1][...] = value.astype(jnp.bfloat16)

    return call_small(
        body, pltpu.VMEM((rank, half), jnp.bfloat16), [*others, couplings, lowers, *fars, after]
    )


def local_part(rounded, own, partner, near, basis_out, leaf_coupling, lowers, local, after):
    tiles, rows, _ = rounded.shape
    columns = tiles * LANES
    leaves, leaf_rows, _ = near.shape
    rank = basis_out.shape[2]
    width = tiles + rank // LANES
    groups = rows // SUBLANES
    chunk = 256
    blocks = rows // chunk

    def body(
        near_hbm,
        rounded_ref,
        own_ref,
        partner_ref,
        basis_ref,
        coupling_ref,
        lower_ref,
        local_ref,
        after_ref,
        initial,
        tree,
        near_ref,
        children,
        order_ref,
        sems,
        order_sem,
    ):
        low = lax.axis_index("gz") & 1
        order_copy = pltpu.make_async_copy(local_ref, order_ref, order_sem)
        order_copy.start()
        copies = [
            pltpu.make_async_copy(near_hbm.at[leaf], near_ref.at[leaf], sems.at[leaf])
            for leaf in range(leaves)
        ]
        for copy in copies:
            copy.start()
        children[pl.ds(low * leaves, leaves)] = own_ref[...]
        children[pl.ds((1 - low) * leaves, leaves)] = partner_ref[...]
        tree_flat = flat(tree)
        initial_flat = flat(initial)
        fars = []

        def keep(first, size, column, value):
            for t in range(value.shape[1] // LANES):
                tree[first // SUBLANES : (first + size) // SUBLANES, column + t] = value[
                    :, t * LANES : (t + 1) * LANES
                ].reshape(size // SUBLANES, SUBLANES, LANES)

        for leaf in range(leaves):
            slot = low * leaves + leaf
            far = None
            for t in range(ARITY - 1):
                source = t + (t >= slot).astype(jnp.int32)
                term = dot(coupling_ref[leaf, t], children[source])
                far = term if far is None else far + term
            fars.append(far.astype(jnp.bfloat16))
            lower = lower_ref[0, 0, pl.ds(pl.multiple_of(slot * rank, rank), rank), :]
            keep(leaf * leaf_rows, leaf_rows, tiles, dot(basis_ref[leaf], lower))
        order_copy.wait()

        def compute(block):
            outer = block * chunk
            leaf = outer // leaf_rows
            inner = outer - leaf * leaf_rows
            if inner == 0:
                copies[leaf].wait()
            values = wide(rounded_ref, leaf * leaf_rows, leaf_rows)
            value = dot(near_ref[leaf, inner : inner + chunk, :], values)
            value = value + dot(basis_ref[leaf, inner : inner + chunk, :], fars[leaf])
            keep(outer, chunk, 0, value)

        def scatter(block):
            for i in range(block * chunk, (block + 1) * chunk):
                initial_flat[pl.ds(order_ref[i], width, stride=SUBLANES), :] = tree_flat[
                    pl.ds(tiled_place(i, width), width, stride=SUBLANES), :
                ]

        for block in range(blocks):
            compute(block)
            if block:
                scatter(block - 1)
        scatter(blocks - 1)

    hbm_spec = pl.BlockSpec(memory_space=pltpu.HBM)
    return pl.pallas_call(
        body,
        name="local_part",
        out_shape=pltpu.VMEM((groups, width, SUBLANES, LANES), jnp.float32),
        in_specs=[hbm_spec] + [vmem_spec()] * 8,
        out_specs=vmem_spec(),
        scratch_shapes=[
            pltpu.VMEM((groups, width, SUBLANES, LANES), jnp.float32),
            pltpu.VMEM(near.shape, near.dtype),
            pltpu.VMEM((ARITY, rank, columns), jnp.bfloat16),
            pltpu.SMEM(local.shape, local.dtype),
            pltpu.SemaphoreType.DMA((leaves,)),
            pltpu.SemaphoreType.DMA,
        ],
        compiler_params=pltpu.CompilerParams(vmem_limit_bytes=16 * MIB),
    )(stay(near), rounded, own, partner, basis_out, leaf_coupling, lowers, local, after)


def to_rows(initial, tiled, ridge, after):
    groups, width, _, _ = initial.shape
    tiles = tiled.shape[1]
    rows = groups * SUBLANES
    rank = (width - tiles) * LANES
    chunk = 256
    size = chunk // SUBLANES

    def body(ridge_ref, initial_ref, tiled_ref, after_ref, base_ref, spread_ref):
        ridge_value = ridge_ref[0]

        def spread(block, _):
            group = pl.ds(block * size, size)
            for t in range(tiles):
                base_ref[group, t] = initial_ref[group, t] + ridge_value * tiled_ref[group, t]
            first = pl.multiple_of(block * chunk, chunk)
            for t in range(width - tiles):
                spread_ref[pl.ds(first, chunk), t * LANES : (t + 1) * LANES] = (
                    initial_ref[group, tiles + t].reshape(chunk, LANES).astype(jnp.bfloat16)
                )
            return 0

        lax.fori_loop(0, rows // chunk, spread, 0)

    smem_spec = pl.BlockSpec(memory_space=pltpu.SMEM)
    return pl.pallas_call(
        body,
        name="to_rows",
        out_shape=[
            pltpu.VMEM(tiled.shape, jnp.float32),
            pltpu.VMEM((rows, rank), jnp.bfloat16),
        ],
        in_specs=[smem_spec] + [vmem_spec()] * 3,
        out_specs=[vmem_spec()] * 2,
        compiler_params=pltpu.CompilerParams(vmem_limit_bytes=4 * MIB),
    )(ridge, initial, tiled, after)


def finish(base, spread, lowered, other, previous):
    groups, tiles, _, _ = base.shape
    rows = groups * SUBLANES
    half = tiles // 2
    parts = 4
    step = rows // parts
    size = step // SUBLANES

    def body(*refs):
        base_ref, spread_ref, lowered_ref = refs[:3]
        out_ref, result, sems = refs[-3:]
        place = lax.axis_index("gz") & 1
        if other:
            place = 1 - place
        copies = []
        for p in range(parts):
            group = slice(p * size, (p + 1) * size)
            value = dot(spread_ref[p * step : (p + 1) * step, :], lowered_ref[...])
            for t in range(half):
                result[t, group] = base_ref[group, place * half + t] + value[
                    :, t * LANES : (t + 1) * LANES
                ].reshape(size, SUBLANES, LANES)
            for t in range(half):
                column = pl.multiple_of((place * half + t) * LANES, LANES)
                copy = pltpu.make_async_copy(
                    result.at[t, pl.ds(p * size, size)],
                    out_ref.at[pl.ds(p * size, size), :, pl.ds(column, LANES)],
                    sems.at[p * half + t],
                )
                copy.start()
                copies.append(copy)
        for copy in copies:
            copy.wait()

    hbm_spec = pl.BlockSpec(memory_space=pltpu.HBM)
    extra = [] if previous is None else [previous]
    return pl.pallas_call(
        body,
        name="finish_other" if other else "finish_own",
        out_shape=pltpu.HBM((groups, SUBLANES, tiles * LANES), jnp.float32),
        in_specs=[vmem_spec()] * 3 + [hbm_spec] * len(extra),
        out_specs=hbm_spec,
        scratch_shapes=[
            pltpu.VMEM((half, groups, SUBLANES, LANES), jnp.float32),
            pltpu.SemaphoreType.DMA((parts * half,)),
        ],
        input_output_aliases={3: 0} if extra else {},
        compiler_params=pltpu.CompilerParams(vmem_limit_bytes=4 * MIB),
    )(base, spread, lowered, *extra)


def swap(value, axis, mask):
    size = lax.axis_size(axis)
    return lax.ppermute(value, axis, [(s, s ^ mask) for s in range(size)])


def swap_siblings(value, axis, number, shift):
    even, odd = steps_of(axis, number)
    if even == odd:
        return swap(value, axis, number << shift)
    cores = lax.axis_size("gz")
    pairs = []
    for s in range(lax.axis_size(axis)):
        for core in range(cores):
            mask = (odd if core & 1 else even) << shift
            pairs.append((s * cores + core, (s ^ mask) * cores + core))
    return lax.ppermute(value, (axis, "gz"), pairs)


def on_device(
    points,
    order,
    near,
    basis_in,
    basis_out,
    leaf_coupling,
    transfer_up,
    transfer_down,
    node_coupling,
    ridge,
):
    stages = transfer_up.shape[1]
    places = [("gz", 1 + 2 * i) for i in range(stages - 2)] + [("gy", 0), ("gx", 0)]
    held = [transfer_up, leaf_coupling, basis_out, transfer_down, node_coupling]
    rounded, leaf_hat, tiled, local, part, sent, *kept = upward_leaves(
        points, order, basis_in, held
    )
    lifters, leaf_couplings, bases, lowers, couplings = kept
    hat = first_sum(part, swap(sent, "gz", 1))
    fars = []
    for stage, (axis, shift) in enumerate(places):
        others = [None] * (ARITY - 1)
        for step in STEPS[axis]:
            others[step - 1] = swap_siblings(hat, axis, step, shift)
        if stage == 0:
            leaf_hat, _ = lax.optimization_barrier((leaf_hat, hat))
            partner_hat = swap(leaf_hat, "gz", 1)
            initial = local_part(
                rounded, leaf_hat, partner_hat, near, bases, leaf_couplings, lowers, local, hat
            )
            after = initial
        if stage == 1:
            base, spread = to_rows(initial, tiled, ridge, hat)
        if stage + 1 < stages:
            hat = next_lift(hat, others, lifters, stage, axis, shift, after)
            after = hat
            fars.append(far_of(others, couplings, stage, axis, shift, hat))
    value = go_down(others, fars, couplings, lowers, places, spread)
    partner_value = swap(value, "gz", 1)
    result = finish(base, spread, value, False, None)
    result = finish(base, spread, partner_value, True, result)
    return result.reshape(points.shape)


def solution(mesh):
    placed = (
        P(("gx", "gy", "gz"), None),
        P(("gx", "gy", "gz")),
        P(("gx", "gy", "gz"), None, None),
        P(("gx", "gy", "gz"), None, None),
        P(("gx", "gy", "gz"), None, None),
        P(("gx", "gy", "gz"), None, None, None),
        P(("gx", "gy", "gz"), None, None, None),
        P(("gx", "gy", "gz"), None, None, None),
        P(("gx", "gy", "gz"), None, None, None, None),
        P(),
    )

    return jax.shard_map(
        on_device,
        mesh=mesh,
        in_specs=placed,
        out_specs=P(("gx", "gy", "gz"), None),
        check_vma=False,
    )
```
